768 devices in a mesh: wide: 96 (over y, z), narrow: 8 (over x, core).
Axes of the slice: x: 4, y: 8, z: 12, core: 2. Of those that a mesh axis runs over, the one named last changes fastest.
Arguments:
- points: bfloat16 [3072, 256, 256], P('wide', 'narrow'), may hold values from -6 to 6
- targets: bfloat16 [3072, 256, 256], P('wide', 'narrow'), may hold values from -6 to 6
- centroids: float32 [1536, 256], P('wide'), may hold values from -3 to 3
- block_list: int32 [3072], P('wide'), may hold values from 0 to 15
- lengths: int32 [3072], P('wide'), may hold values from 1 to 256
- sources: int32 [3072], P('wide'), may hold values from 0 to 3071, as said below
Outputs:
- rotated: bfloat16 [3072, 256, 256], P('wide', 'narrow')
The draws below stay inside these ranges and needn't reach their ends.
Inputs may be any that keep to these rules, and one draw needn't show every extreme that they name: For every index w of wide and slot j below 2, sources[w * 32 + j] = u * 32 + j for some index u of wide, each such input block named exactly once; every other entry names its own position.
All inputs are finite; a program needn't handle non-finite values.
Results may differ from the reference program's by a relative error of at most 0.0051.
Values may be sent and summed in bfloat16 or wider, within the bound.
A program may use at most 32 MiB of HBM per device.

```python
import math
import jax
import jax.numpy as jnp
import numpy as np
from jax import lax

D = 256
LIST_DEV = 16
BLK = 256
BLK_DEV = 32
MOVE = 2
ITERS = 5
NBLK = 3072
LISTS = 1536


def draw_sources(key, part):
    groups = NBLK // BLK_DEV
    table = jnp.arange(NBLK, dtype=jnp.int32).reshape(groups, BLK_DEV)
    for slot_index in range(MOVE):
        donors = jax.random.permutation(jax.random.fold_in(key, 17 + slot_index), groups).astype(jnp.int32)
        table = table.at[:, slot_index].set(donors * BLK_DEV + slot_index)
    return table.reshape(NBLK)


def with_ends(drawn, stream_key, least, high):
    longest = drawn.shape.index(max(drawn.shape))
    spots = []
    for shift in (0, 1):
        where = [jax.random.randint(jax.random.fold_in(stream_key, axis), (), 0, length) for axis, length in enumerate(drawn.shape)]
        where[longest] = (where[longest] + shift) % drawn.shape[longest]
        spots.append(tuple(where))
    return drawn.at[spots[0]].set(least).at[spots[1]].set(high)


def block_levels(stream_key, shape, pieces, least, top_value):
    level, own = 1.0, jax.random.fold_in(stream_key, 6)
    for axis_at, parts in pieces:
        heights = jnp.exp(jax.random.uniform(jax.random.fold_in(own, axis_at), (parts,), jnp.float32, least / len(pieces), top_value / len(pieces)))
        level = level * jnp.repeat(heights, shape[axis_at] // parts).reshape([-1 if axis == axis_at else 1 for axis in range(len(shape))])
    return level


def cumulative_ranks(count, slope):
    portions = [(1 << 20) // math.isqrt(standing ** slope) + 1 for standing in range(1, count + 1)]
    width = 1 + sum(portions) // (1 << 30)
    return np.cumsum(np.array([max(1, weight // width) for weight in portions]))


def skewed_ids(key, extent, amount, skew):
    table = cumulative_ranks(amount, skew)
    ticket = jax.random.randint(jax.random.fold_in(key, 1), extent, 0, int(table[amount - 1]))
    standing = jnp.searchsorted(jnp.asarray(table, jnp.int32), ticket, side="right")
    return jax.random.permutation(jax.random.fold_in(key, 2), amount)[standing].astype(jnp.int32)


def centred(key, extent, spread, reach, split=(), held_as=jnp.bfloat16):
    result = jax.random.normal(key, extent, jnp.float32) * spread
    if len(split) > 0:
        result = block_levels(key, extent, split, -0.22, 0.18) * result
    return jnp.clip(result, min=-reach, max=reach).astype(held_as)


def setup_inputs(seed: int = 0) -> dict:
    splits = jax.random.split(jax.random.key(seed), 7)
    points = centred(splits[0], (NBLK, BLK, D), 1.0, 6.0, ((0, 96), (1, 8)))
    targets = centred(splits[1], (NBLK, BLK, D), 1.0, 6.0, ((0, 96), (1, 8)))
    centroids = centred(splits[2], (LISTS, D), 0.5, 3.0, ((0, 96),), jnp.float32)
    block_list = with_ends(skewed_ids(splits[3], (NBLK,), LIST_DEV, 2), jax.random.fold_in(splits[3], 3), 0, LIST_DEV - 1).astype(jnp.int32)
    lengths = with_ends(jax.random.randint(splits[4], (NBLK,), 1, BLK + 1), jax.random.fold_in(splits[4], 1), 1, BLK).astype(jnp.int32)
    sources = draw_sources(jax.random.fold_in(splits[6], 71), 0)
    return dict(points=points, targets=targets, centroids=centroids, block_list=block_list, lengths=lengths, sources=sources)


highest_prec = lax.Precision.HIGHEST

def newton_polar(cross_gram):
    frob_norm = jnp.sqrt(lax.optimization_barrier(jnp.sum(cross_gram * cross_gram, axis=(1, 2), keepdims=True)) + 1e-06)
    polar_iter = cross_gram / frob_norm
    for sweep_index in range(ITERS):
        product = jnp.einsum('lde,lfe->ldf', polar_iter, polar_iter, precision=highest_prec)
        polar_iter = 1.5 * polar_iter - 0.5 * jnp.einsum('ldf,lfe->lde', product, polar_iter, precision=highest_prec)
    return polar_iter.astype(jnp.bfloat16)

def one_group(group):
    points, targets, centroids, block_list, lengths = group
    list_pick = (block_list[:, None] == jnp.arange(LIST_DEV, dtype=jnp.int32)[None, :]).astype(jnp.float32)
    centre_rows = jnp.dot(list_pick, centroids, precision=highest_prec)
    in_range = jnp.arange(BLK, dtype=jnp.int32)[None, :] < lengths[:, None]
    residual = jnp.where(in_range[:, :, None], points.astype(jnp.float32) - centre_rows[:, None, :], 0.0).astype(jnp.bfloat16)
    block_grams = jnp.einsum('brd,bre->bde', residual.astype(jnp.float32), targets.astype(jnp.float32), precision=highest_prec)
    cross_gram = jnp.einsum('bl,bde->lde', list_pick, block_grams, precision=highest_prec)
    rotation = newton_polar(cross_gram)
    chosen = jnp.einsum('bl,lde->bde', list_pick, rotation.astype(jnp.float32), precision=highest_prec)
    turned = jnp.einsum('brd,bde->bre', residual.astype(jnp.float32), chosen, precision=highest_prec)
    return turned.astype(jnp.bfloat16)

def reference(points, targets, centroids, block_list, lengths, sources):
    groups = NBLK // BLK_DEV
    shaped = (points.reshape(groups, BLK_DEV, BLK, D), targets.reshape(groups, BLK_DEV, BLK, D), centroids.reshape(groups, LIST_DEV, D), block_list.reshape(groups, BLK_DEV), lengths.reshape(groups, BLK_DEV))
    turned = lax.map(one_group, shaped).reshape(NBLK, BLK, D)
    return jnp.take(turned, sources, axis=0)
```

```python
import functools

import jax
import jax.numpy as jnp
from jax import lax
from jax.experimental import pallas as pl
from jax.experimental.pallas import tpu as pltpu
from jax.sharding import PartitionSpec as P

MOVE = 2
SWEEPS = 5
CHIPS_X = 4
RING_Y = 8
RING_Z = 12
PER_DEV = 2

MESH = pl.DeviceIdType.MESH
BF16 = jnp.bfloat16
F32 = jnp.float32


def mm(a, b):
    return jnp.dot(a, b, preferred_element_type=F32)


def mm_nt(a, b):
    return lax.dot_general(a, b, (((1,), (1,)), ((), ())), preferred_element_type=F32)


def split_bf16(a):
    high = a.astype(BF16)
    return high, (a - high.astype(F32)).astype(BF16)


def remote(src, dst, send_sem, recv_sem, where):
    return pltpu.make_async_remote_copy(
        src_ref=src,
        dst_ref=dst,
        send_sem=send_sem,
        recv_sem=recv_sem,
        device_id=where,
        device_id_type=MESH,
    )


def x_partners(narrow):
    chip, core = narrow // 2, narrow % 2
    right = ((chip + 1) % CHIPS_X) * 2 + core
    left = ((chip + CHIPS_X - 1) % CHIPS_X) * 2 + core
    sibling = chip * 2 + 1 - core
    return chip, core, right, left, sibling


def reduce_kernel(
    blocks,
    rows,
    points,
    targets,
    centroids,
    block_list,
    lengths,
    gram_out,
    res_own,
    own_p,
    own_t,
    sib_p,
    sib_t,
    res_sib,
    turned_t,
    masked,
    kept,
    out_buf,
    in_buf,
    load_sem,
    send_sem,
    recv_sem,
):
    narrow = lax.axis_index("narrow")
    chip, core, right, left, sibling = x_partners(narrow)
    width = points.shape[1]
    total = blocks * rows

    load_t = pltpu.make_async_copy(targets, own_t, load_sem.at[0])
    load_p = pltpu.make_async_copy(points, own_p, load_sem.at[1])
    load_t.start()
    load_p.start()

    barrier = pltpu.get_barrier_semaphore()
    for partner in (sibling, right, left):
        pl.semaphore_signal(barrier, inc=1, device_id={"narrow": partner}, device_id_type=MESH)
    pl.semaphore_wait(barrier, 3)

    swap_t = remote(targets, sib_t, send_sem.at[6], recv_sem.at[6], {"narrow": sibling})
    swap_p = remote(points, sib_p, send_sem.at[7], recv_sem.at[7], {"narrow": sibling})
    swap_t.start()
    swap_p.start()

    def residual_into(dst, src, first_row):
        def one(b, carry):
            base = pl.multiple_of(b * rows, rows)
            centre = centroids[pl.ds(block_list[b], 1), :]
            row = first_row + lax.broadcasted_iota(jnp.int32, (rows, width), 0)
            value = src[pl.ds(base, rows), :].astype(F32) - centre
            dst[pl.ds(base, rows), :] = jnp.where(row < lengths[b], value, 0.0).astype(BF16)
            return carry

        lax.fori_loop(0, blocks, one, 0, unroll=4)

    def transpose_into(first, src):
        for piece in range(total // width):
            turned_t[:, first + piece * width : first + (piece + 1) * width] = src[
                piece * width : (piece + 1) * width, :
            ].T

    load_t.wait()
    transpose_into(0, own_t)
    load_p.wait()
    residual_into(res_own, own_p, narrow * rows)
    swap_t.wait_recv()
    transpose_into(total, sib_t)
    swap_p.wait_recv()
    residual_into(res_sib, sib_p, sibling * rows)

    def gram(owner_chip, which, slot):
        wanted = (owner_chip * 2 + core) * PER_DEV + which

        def one(b, carry):
            base = pl.multiple_of(b * rows, rows)
            keep = jnp.where(block_list[b] == wanted, 1.0, 0.0).astype(BF16)
            masked[slot, pl.ds(base, rows), :] = res_own[pl.ds(base, rows), :] * keep
            masked[slot, pl.ds(total + base, rows), :] = res_sib[pl.ds(base, rows), :] * keep
            return carry

        lax.fori_loop(0, blocks, one, 0, unroll=8)
        return mm(turned_t[...], masked[slot])

    opposite = (chip + 2) % CHIPS_X
    right_chip = (chip + 1) % CHIPS_X
    left_chip = (chip + CHIPS_X - 1) % CHIPS_X

    def hop(slot, where):
        return remote(
            out_buf.at[slot], in_buf.at[slot], send_sem.at[slot], recv_sem.at[slot], {"narrow": where}
        )

    hops = [hop(s, right if s % 2 == 0 else left) for s in range(6)]
    out_buf[0] = gram(opposite, 0, 0).astype(BF16)
    hops[0].start()
    out_buf[1] = gram(opposite, 1, 1).astype(BF16)
    hops[1].start()
    out_buf[2] = gram(right_chip, 1, 0).astype(BF16)
    hops[2].start()
    out_buf[3] = gram(left_chip, 0, 1).astype(BF16)
    hops[3].start()
    kept[0] = gram(right_chip, 0, 0)
    kept[1] = gram(left_chip, 1, 1)
    kept[2] = gram(chip, 0, 0)
    kept[3] = gram(chip, 1, 1)
    hops[0].wait_recv()
    out_buf[4] = (kept[0] + in_buf[0].astype(F32)).astype(BF16)
    hops[4].start()
    hops[1].wait_recv()
    out_buf[5] = (kept[1] + in_buf[1].astype(F32)).astype(BF16)
    hops[5].start()
    hops[3].wait_recv()
    kept[2] = kept[2] + in_buf[3].astype(F32)
    hops[2].wait_recv()
    kept[3] = kept[3] + in_buf[2].astype(F32)
    hops[4].wait_recv()
    gram_out[0] = kept[2] + in_buf[4].astype(F32)
    hops[5].wait_recv()
    gram_out[1] = kept[3] + in_buf[5].astype(F32)
    for copy in hops:
        copy.wait_send()
    swap_t.wait_send()
    swap_p.wait_send()


def turn_kernel(
    blocks,
    rows,
    gram_in,
    res,
    block_list,
    sources,
    out,
    iterate,
    rot,
    hand0,
    hand1,
    got_z,
    got_y,
    pass_y,
    pass_z,
    last_y,
    last_z,
    ask,
    ask_y,
    ask_z,
    read_y,
    read_z,
    rot_send,
    rot_recv,
    ask_sy,
    ask_sz,
    ask_ry,
    ask_rz,
    g_sz,
    g_rz,
    g_sy,
    g_ry,
    p_sy,
    p_ry,
    p_sz,
    p_rz,
    read_sem,
):
    wide = lax.axis_index("wide")
    narrow = lax.axis_index("narrow")
    at_y, at_z = wide // RING_Z, wide % RING_Z
    chip, core, right, left, sibling = x_partners(narrow)

    def y_peer(step):
        other = (at_y + step) % RING_Y
        return other, {"wide": other * RING_Z + at_z}

    def z_peer(step):
        other = (at_z + step) % RING_Z
        return other, {"wide": at_y * RING_Z + other}

    y_steps = sorted(range(1, RING_Y), key=lambda s: -min(s, RING_Y - s))
    z_steps = sorted(range(1, RING_Z), key=lambda s: -min(s, RING_Z - s))

    barrier = pltpu.get_barrier_semaphore()
    for step in z_steps:
        pl.semaphore_signal(barrier, inc=1, device_id=z_peer(step)[1], device_id_type=MESH)
    for step in y_steps:
        pl.semaphore_signal(barrier, inc=1, device_id=y_peer(step)[1], device_id_type=MESH)
    for partner in (sibling, right, left):
        pl.semaphore_signal(barrier, inc=1, device_id={"narrow": partner}, device_id_type=MESH)

    line = lax.broadcasted_iota(jnp.int32, ask.shape, 0)
    ask[...] = jnp.where(line == 0, sources[0], sources[1])
    ask_y[at_y] = ask[...]
    ask_z[at_z] = ask[...]

    for which in range(PER_DEV):
        gram = gram_in[which]
        norm = jnp.sqrt(jnp.sum(gram * gram, keepdims=True) + 1e-06)
        iterate[which] = gram / norm

    def sweep(index, carry):
        for which in range(PER_DEV):
            held = iterate[which].astype(BF16)
            product = mm_nt(held, held).astype(BF16)
            iterate[which] = 1.5 * iterate[which] - 0.5 * mm(product, held)
        return carry

    lax.fori_loop(0, SWEEPS - 1, sweep, 0)
    for which in range(PER_DEV):
        exact = iterate[which]
        high, low = split_bf16(exact)
        product = mm_nt(high, high) + (mm_nt(high, low) + mm_nt(low, high))
        p_high, p_low = split_bf16(product)
        cubed = mm(p_high, high) + (mm(p_high, low) + mm(p_low, high))
        rot[narrow * PER_DEV + which] = (1.5 * exact - 0.5 * cubed).astype(BF16)

    pl.semaphore_wait(barrier, RING_Y - 1 + RING_Z - 1 + 3)

    right_chip = (chip + 1) % CHIPS_X
    left_chip = (chip + CHIPS_X - 1) % CHIPS_X
    opposite = (chip + 2) % CHIPS_X

    def place(owner_chip, owner_core, which):
        return (owner_chip * 2 + owner_core) * PER_DEV + which

    sent = []

    def share(slot, where):
        copy = remote(
            rot.at[slot], rot.at[slot], rot_send.at[len(sent)], rot_recv.at[slot], {"narrow": where}
        )
        copy.start()
        sent.append(copy)

    def arrived(slot):
        remote(rot.at[slot], rot.at[slot], rot_send.at[0], rot_recv.at[slot], {"narrow": sibling}).wait_recv()

    share(place(chip, core, 0), right)
    share(place(chip, core, 1), left)
    share(place(chip, core, 1), right)
    share(place(chip, core, 0), left)
    share(place(chip, core, 0), sibling)
    share(place(chip, core, 1), sibling)

    asks = []
    for step in y_steps:
        other, where = y_peer(step)
        copy = remote(ask, ask_y.at[at_y], ask_sy.at[step], ask_ry.at[at_y], where)
        copy.start()
        asks.append(copy)
    for step in z_steps:
        other, where = z_peer(step)
        copy = remote(ask, ask_z.at[at_z], ask_sz.at[step], ask_rz.at[at_z], where)
        copy.start()
        asks.append(copy)

    arrived(place(left_chip, core, 0))
    share(place(left_chip, core, 0), right)
    share(place(left_chip, core, 0), sibling)
    arrived(place(right_chip, core, 1))
    share(place(right_chip, core, 1), left)
    share(place(right_chip, core, 1), sibling)
    arrived(place(left_chip, core, 1))
    share(place(left_chip, core, 1), sibling)
    arrived(place(right_chip, core, 0))
    share(place(right_chip, core, 0), sibling)

    for step in y_steps:
        other, where = y_peer(step)
        remote(ask, ask_y.at[other], ask_sy.at[step], ask_ry.at[other], where).wait_recv()
    for step in z_steps:
        other, where = z_peer(step)
        remote(ask, ask_z.at[other], ask_sz.at[step], ask_rz.at[other], where).wait_recv()
    to_scalars_y = pltpu.make_async_copy(ask_y, read_y, read_sem.at[0])
    to_scalars_z = pltpu.make_async_copy(ask_z, read_z, read_sem.at[1])
    to_scalars_y.start()
    to_scalars_z.start()
    to_scalars_y.wait()
    to_scalars_z.wait()

    arrived(place(opposite, core, 0))
    share(place(opposite, core, 0), sibling)
    arrived(place(opposite, core, 1))
    share(place(opposite, core, 1), sibling)
    for owner_chip in (chip, left_chip, right_chip, opposite):
        for which in range(PER_DEV):
            arrived(place(owner_chip, 1 - core, which))

    def turn(b):
        base = pl.multiple_of(b * rows, rows)
        return mm_nt(res[pl.ds(base, rows), :], rot[block_list[b]]).astype(BF16)

    first, second = turn(0), turn(1)
    hand0[...] = first
    hand1[...] = second
    got_z[at_z] = first
    got_y[at_y] = second
    moves = []
    for step in z_steps:
        other, where = z_peer(step)
        copy = remote(hand0, got_z.at[at_z], g_sz.at[step], g_rz.at[at_z], where)
        copy.start()
        moves.append(copy)
    for step in y_steps:
        other, where = y_peer(step)
        copy = remote(hand1, got_y.at[at_y], g_sy.at[step], g_ry.at[at_y], where)
        copy.start()
        moves.append(copy)

    def turn_one(b, carry):
        out[pl.ds(pl.multiple_of(b * rows, rows), rows), :] = turn(b)
        return carry

    lax.fori_loop(MOVE, blocks, turn_one, 0, unroll=2)

    def from_y(source):
        return source // blocks // RING_Z

    def from_z(source):
        return source // blocks % RING_Z

    for step in y_steps:
        other, where = y_peer(step)
        remote(hand1, got_y.at[other], g_sy.at[step], g_ry.at[other], where).wait_recv()
    last_z[at_z] = got_y[from_y(sources[1])]
    for step in z_steps:
        other, where = z_peer(step)
        pass_z[other] = got_y[from_y(read_z[other, 1, 0])]
        copy = remote(pass_z.at[other], last_z.at[at_z], p_sz.at[step], p_rz.at[at_z], where)
        copy.start()
        moves.append(copy)

    for step in z_steps:
        other, where = z_peer(step)
        remote(hand0, got_z.at[other], g_sz.at[step], g_rz.at[other], where).wait_recv()
    last_y[at_y] = got_z[from_z(sources[0])]
    for step in y_steps:
        other, where = y_peer(step)
        pass_y[other] = got_z[from_z(read_y[other, 0, 0])]
        copy = remote(pass_y.at[other], last_y.at[at_y], p_sy.at[step], p_ry.at[at_y], where)
        copy.start()
        moves.append(copy)

    for step in y_steps:
        other, where = y_peer(step)
        remote(hand1, last_y.at[other], p_sy.at[step], p_ry.at[other], where).wait_recv()
    out[0:rows, :] = last_y[from_y(sources[0])]
    for step in z_steps:
        other, where = z_peer(step)
        remote(hand0, last_z.at[other], p_sz.at[step], p_rz.at[other], where).wait_recv()
    out[rows : 2 * rows, :] = last_z[from_z(sources[1])]

    for copy in sent + asks + moves:
        copy.wait_send()


def local(points, targets, centroids, block_list, lengths, sources):
    blocks, rows, width = points.shape
    lists = centroids.shape[0]
    total = blocks * rows
    vmem = pl.BlockSpec(memory_space=pltpu.VMEM)
    smem = pl.BlockSpec(memory_space=pltpu.SMEM)
    anywhere = pl.BlockSpec(memory_space=pl.ANY)
    dma = pltpu.SemaphoreType.DMA
    square = (width, width)
    gram, residual = pl.pallas_call(
        functools.partial(reduce_kernel, blocks, rows),
        out_shape=(
            jax.ShapeDtypeStruct((PER_DEV, *square), F32),
            jax.ShapeDtypeStruct((total, width), BF16),
        ),
        in_specs=[anywhere, anywhere, vmem, smem, smem],
        out_specs=(vmem, vmem),
        scratch_shapes=[
            pltpu.VMEM((total, width), BF16),
            pltpu.VMEM((total, width), BF16),
            pltpu.VMEM((total, width), BF16),
            pltpu.VMEM((total, width), BF16),
            pltpu.VMEM((total, width), BF16),
            pltpu.VMEM((width, 2 * total), BF16),
            pltpu.VMEM((2, 2 * total, width), BF16),
            pltpu.VMEM((4, *square), F32),
            pltpu.VMEM((6, *square), BF16),
            pltpu.VMEM((6, *square), BF16),
            dma((2,)),
            dma((8,)),
            dma((8,)),
        ],
        compiler_params=pltpu.CompilerParams(collective_id=0, has_side_effects=True),
        name="reduce_grams",
    )(
        points.reshape(total, width),
        targets.reshape(total, width),
        centroids,
        block_list,
        lengths,
    )
    tile = (rows, width)
    ask = (8, 128)
    rotated = pl.pallas_call(
        functools.partial(turn_kernel, blocks, rows),
        out_shape=jax.ShapeDtypeStruct((total, width), BF16),
        in_specs=[vmem, vmem, smem, smem],
        out_specs=vmem,
        scratch_shapes=[
            pltpu.VMEM((PER_DEV, *square), F32),
            pltpu.VMEM((lists, *square), BF16),
            pltpu.VMEM(tile, BF16),
            pltpu.VMEM(tile, BF16),
            pltpu.VMEM((RING_Z, *tile), BF16),
            pltpu.VMEM((RING_Y, *tile), BF16),
            pltpu.VMEM((RING_Y, *tile), BF16),
            pltpu.VMEM((RING_Z, *tile), BF16),
            pltpu.VMEM((RING_Y, *tile), BF16),
            pltpu.VMEM((RING_Z, *tile), BF16),
            pltpu.VMEM(ask, jnp.int32),
            pltpu.VMEM((RING_Y, *ask), jnp.int32),
            pltpu.VMEM((RING_Z, *ask), jnp.int32),
            pltpu.SMEM((RING_Y, *ask), jnp.int32),
            pltpu.SMEM((RING_Z, *ask), jnp.int32),
            dma((14,)),
            dma((lists,)),
            dma((RING_Y,)),
            dma((RING_Z,)),
            dma((RING_Y,)),
            dma((RING_Z,)),
            dma((RING_Z,)),
            dma((RING_Z,)),
            dma((RING_Y,)),
            dma((RING_Y,)),
            dma((RING_Y,)),
            dma((RING_Y,)),
            dma((RING_Z,)),
            dma((RING_Z,)),
            dma((2,)),
        ],
        compiler_params=pltpu.CompilerParams(collective_id=1, has_side_effects=True),
        name="turn_and_hand",
    )(gram, residual, block_list, sources)
    return rotated.reshape(blocks, rows, width)


def solution(mesh):
    return jax.shard_map(
        local,
        mesh=mesh,
        in_specs=(
            P("wide", "narrow", None),
            P("wide", "narrow", None),
            P("wide", None),
            P("wide"),
            P("wide"),
            P("wide"),
        ),
        out_specs=P("wide", "narrow", None),
        check_vma=False,
    )
```

```python
import functools

import jax
import jax.numpy as jnp
from jax import lax
from jax.experimental import pallas as pl
from jax.experimental.pallas import tpu as pltpu
from jax.sharding import PartitionSpec as P

MOVE = 2
SWEEPS = 5
CHIPS_X = 4
RING_Y = 8
RING_Z = 12
PER_DEV = 2

MESH = pl.DeviceIdType.MESH
BF16 = jnp.bfloat16
F32 = jnp.float32


def mm(a, b):
    return jnp.dot(a, b, preferred_element_type=F32)


def mm_nt(a, b):
    return lax.dot_general(a, b, (((1,), (1,)), ((), ())), preferred_element_type=F32)


def split_bf16(a):
    high = a.astype(BF16)
    return high, (a - high.astype(F32)).astype(BF16)


def remote(src, dst, send_sem, recv_sem, where):
    return pltpu.make_async_remote_copy(
        src_ref=src,
        dst_ref=dst,
        send_sem=send_sem,
        recv_sem=recv_sem,
        device_id=where,
        device_id_type=MESH,
    )


def x_partners(narrow):
    chip, core = narrow // 2, narrow % 2
    right = ((chip + 1) % CHIPS_X) * 2 + core
    left = ((chip + CHIPS_X - 1) % CHIPS_X) * 2 + core
    sibling = chip * 2 + 1 - core
    return chip, core, right, left, sibling


def kernel(
    blocks,
    rows,
    points,
    targets,
    centroids_hbm,
    block_list_hbm,
    lengths_hbm,
    sources_hbm,
    out,
    centroids,
    block_list,
    lengths,
    sources,
    own_p,
    own_t,
    sib_p,
    sib_t,
    res,
    res_sib,
    turned_t,
    kept,
    out_buf,
    in_buf,
    raw,
    hand_res,
    iterate,
    mine,
    rot,
    swap_out,
    swap_in,
    hand0,
    hand1,
    got_z,
    got_y,
    pass_y,
    pass_z,
    last_y,
    last_z,
    ask,
    ask_y,
    ask_z,
    read_y,
    read_z,
    load_sem,
    swap_send,
    swap_recv,
    raw_send,
    raw_recv,
    gram_send,
    gram_recv,
    x_send,
    x_recv,
    rot_send,
    rot_recv,
    ask_sy,
    ask_sz,
    ask_ry,
    ask_rz,
    g_sz,
    g_rz,
    g_sy,
    g_ry,
    p_sy,
    p_ry,
    p_sz,
    p_rz,
    read_sem,
    near_sem,
):
    wide = lax.axis_index("wide")
    narrow = lax.axis_index("narrow")
    at_y, at_z = wide // RING_Z, wide % RING_Z
    chip, core, right, left, sibling = x_partners(narrow)
    right_chip = (chip + 1) % CHIPS_X
    left_chip = (chip + CHIPS_X - 1) % CHIPS_X
    opposite = (chip + 2) % CHIPS_X
    width = points.shape[1]
    total = blocks * rows
    handed = MOVE * rows

    def y_peer(step):
        other = (at_y + step) % RING_Y
        return other, {"wide": other * RING_Z + at_z}

    def z_peer(step):
        other = (at_z + step) % RING_Z
        return other, {"wide": at_y * RING_Z + other}

    y_steps = sorted(range(1, RING_Y), key=lambda s: -min(s, RING_Y - s))
    z_steps = sorted(range(1, RING_Z), key=lambda s: -min(s, RING_Z - s))
    around = (
        y_peer(1)[1],
        y_peer(RING_Y - 1)[1],
        z_peer(1)[1],
        z_peer(RING_Z - 1)[1],
    )

    barrier = pltpu.get_barrier_semaphore()
    for partner in (sibling, right, left):
        pl.semaphore_signal(barrier, inc=1, device_id={"narrow": partner}, device_id_type=MESH)
    for where in around:
        pl.semaphore_signal(barrier, inc=1, device_id=where, device_id_type=MESH)

    loads = [
        pltpu.make_async_copy(source, target, load_sem.at[index])
        for index, (source, target) in enumerate(
            (
                (targets, own_t),
                (points, own_p),
                (block_list_hbm, block_list),
                (lengths_hbm, lengths),
                (centroids_hbm, centroids),
                (sources_hbm, sources),
            )
        )
    ]
    for load in loads:
        load.start()
    pl.semaphore_wait(barrier, 3 + len(around))

    swap_t = remote(targets, sib_t, swap_send.at[0], swap_recv.at[0], {"narrow": sibling})
    swap_p = remote(points, sib_p, swap_send.at[1], swap_recv.at[1], {"narrow": sibling})
    swap_t.start()
    swap_p.start()
    sent = [swap_t, swap_p]

    raws = []

    def share_raw(src, owner, where):
        copy = remote(src, raw.at[owner], raw_send.at[len(raws)], raw_recv.at[owner], {"narrow": where})
        copy.start()
        raws.append(copy)

    def raw_arrived(owner):
        remote(
            raw.at[owner], raw.at[owner], raw_send.at[0], raw_recv.at[owner], {"narrow": sibling}
        ).wait_recv()

    share_raw(points.at[pl.ds(0, handed)], narrow, right)
    share_raw(points.at[pl.ds(0, handed)], narrow, left)

    def tell():
        for index, where in enumerate(around):
            pl.semaphore_signal(near_sem.at[index], inc=1, device_id=where, device_id_type=MESH)

    def tell_z():
        for index in (2, 3):
            pl.semaphore_signal(near_sem.at[index], inc=1, device_id=around[index], device_id_type=MESH)

    def hear(kinds):
        for index in kinds:
            pl.semaphore_wait(near_sem.at[index], 1)

    tell()

    def residual_of(value, block, first_row):
        centre = centroids[pl.ds(block_list[block], 1), :]
        row = first_row + lax.broadcasted_iota(jnp.int32, (rows, width), 0)
        return jnp.where(row < lengths[block], value.astype(F32) - centre, 0.0).astype(BF16)

    def residual_into(dst, src, first_row):
        def one(b, carry):
            here = pl.ds(pl.multiple_of(b * rows, rows), rows)
            dst[here, :] = residual_of(src[here, :], b, first_row)
            return carry

        lax.fori_loop(0, blocks, one, 0, unroll=4)

    def transpose_into(first, src):
        for piece in range(total // width):
            turned_t[:, first + piece * width : first + (piece + 1) * width] = src[
                piece * width : (piece + 1) * width, :
            ].T

    loads[0].wait()
    transpose_into(0, own_t)
    for load in loads[1:]:
        load.wait()
    residual_into(res, own_p, narrow * rows)
    swap_t.wait_recv()
    transpose_into(total, sib_t)
    swap_p.wait_recv()
    raw_arrived(left)
    share_raw(raw.at[left], left, right)
    residual_into(res_sib, sib_p, sibling * rows)

    def gram(owner_chip, which):
        wanted = (owner_chip * 2 + core) * PER_DEV + which
        pieces = []
        for held in (res, res_sib):
            for b in range(blocks):
                keep = jnp.where(block_list[b] == wanted, 1.0, 0.0).astype(BF16)
                pieces.append(held[b * rows : (b + 1) * rows, :] * keep)
        return mm(turned_t[...], jnp.concatenate(pieces, axis=0))

    def hop(slot, where):
        return remote(
            out_buf.at[slot], in_buf.at[slot], gram_send.at[slot], gram_recv.at[slot], {"narrow": where}
        )

    hops = [hop(s, right if s % 2 == 0 else left) for s in range(6)]
    sent += hops
    out_buf[0] = gram(opposite, 0).astype(BF16)
    hops[0].start()
    out_buf[1] = gram(opposite, 1).astype(BF16)
    hops[1].start()
    hear((0, 1, 2, 3))
    tell()
    out_buf[2] = gram(right_chip, 1).astype(BF16)
    hops[2].start()
    share_raw(raw.at[left], left, sibling)
    raw_arrived(right)
    share_raw(raw.at[right], right, sibling)
    out_buf[3] = gram(left_chip, 0).astype(BF16)
    hops[3].start()
    hear((0, 1, 2, 3))
    tell()
    kept[0] = gram(right_chip, 0)
    kept[1] = gram(left_chip, 1)
    hear((0, 1, 2, 3))
    tell_z()
    across = opposite * 2 + core
    raw_arrived(across)
    share_raw(raw.at[across], across, sibling)
    kept[2] = gram(chip, 0)
    hear((2, 3))
    tell_z()
    kept[3] = gram(chip, 1)
    hear((2, 3))

    line = lax.broadcasted_iota(jnp.int32, ask.shape, 0)
    wish = jnp.where(line == 0, sources[0], sources[1])
    ask[...] = wish
    ask_y[at_y] = wish
    ask_z[at_z] = wish

    hops[0].wait_recv()
    out_buf[4] = (kept[0] + in_buf[0].astype(F32)).astype(BF16)
    hops[4].start()
    hops[1].wait_recv()
    out_buf[5] = (kept[1] + in_buf[1].astype(F32)).astype(BF16)
    hops[5].start()

    for step in y_steps:
        other, where = y_peer(step)
        copy = remote(ask, ask_y.at[at_y], ask_sy.at[step], ask_ry.at[at_y], where)
        copy.start()
        sent.append(copy)
    for step in z_steps:
        other, where = z_peer(step)
        copy = remote(ask, ask_z.at[at_z], ask_sz.at[step], ask_rz.at[at_z], where)
        copy.start()
        sent.append(copy)

    for b in range(MOVE):
        hand_res[b, pl.ds(pl.multiple_of(narrow * rows, rows), rows), :] = res[
            b * rows : (b + 1) * rows, :
        ]
        hand_res[b, pl.ds(pl.multiple_of(sibling * rows, rows), rows), :] = res_sib[
            b * rows : (b + 1) * rows, :
        ]
    for owner_chip in (left_chip, right_chip, opposite):
        raw_arrived(owner_chip * 2 + 1 - core)
        for owner_core in range(2):
            owner = owner_chip * 2 + owner_core
            for b in range(MOVE):
                hand_res[b, pl.ds(pl.multiple_of(owner * rows, rows), rows), :] = residual_of(
                    raw[owner, b * rows : (b + 1) * rows, :], b, owner * rows
                )

    hops[3].wait_recv()
    kept[2] = kept[2] + in_buf[3].astype(F32)
    hops[2].wait_recv()
    kept[3] = kept[3] + in_buf[2].astype(F32)
    hops[4].wait_recv()
    hops[5].wait_recv()
    for which in range(PER_DEV):
        total_gram = kept[2 + which] + in_buf[4 + which].astype(F32)
        norm = jnp.sqrt(jnp.sum(total_gram * total_gram, keepdims=True) + 1e-06)
        iterate[which] = total_gram / norm

    def sweep(index, carry):
        for which in range(PER_DEV):
            held = iterate[which].astype(BF16)
            product = mm_nt(held, held).astype(BF16)
            iterate[which] = 1.5 * iterate[which] - 0.5 * mm(product, held)
        return carry

    lax.fori_loop(0, SWEEPS - 1, sweep, 0)
    for which in range(PER_DEV):
        exact = iterate[which]
        high, low = split_bf16(exact)
        product = mm_nt(high, high) + (mm_nt(high, low) + mm_nt(low, high))
        p_high, p_low = split_bf16(product)
        cubed = mm(p_high, high) + (mm(p_high, low) + mm(p_low, high))
        rotation = (1.5 * exact - 0.5 * cubed).astype(BF16)
        mine[which] = rotation
        rot[narrow * PER_DEV + which] = rotation

    x_moves = []
    for b in range(MOVE):
        chosen = mine[block_list[b] % PER_DEV]
        swap_out[:, b * rows : (b + 1) * rows, :] = (
            mm_nt(hand_res[b], chosen).astype(BF16).reshape(2 * CHIPS_X, rows, width)
        )
    swap_in[narrow] = swap_out[narrow]
    for chip_step, flip in ((2, 0), (2, 1), (1, 0), (1, 1), (3, 0), (3, 1), (0, 1)):
        peer_core = core + flip - 2 * core * flip
        peer = ((chip + chip_step) % CHIPS_X) * 2 + peer_core
        copy = remote(
            swap_out.at[peer], swap_in.at[narrow], x_send.at[peer], x_recv.at[narrow], {"narrow": peer}
        )
        copy.start()
        x_moves.append((copy, peer))
    sent += [copy for copy, peer in x_moves]

    def place(owner_chip, owner_core, which):
        return (owner_chip * 2 + owner_core) * PER_DEV + which

    shares = []

    def share(slot, where):
        copy = remote(
            rot.at[slot], rot.at[slot], rot_send.at[len(shares)], rot_recv.at[slot], {"narrow": where}
        )
        copy.start()
        shares.append(copy)

    def arrived(slot):
        remote(rot.at[slot], rot.at[slot], rot_send.at[0], rot_recv.at[slot], {"narrow": sibling}).wait_recv()

    share(place(chip, core, 0), right)
    share(place(chip, core, 1), left)
    share(place(chip, core, 1), right)
    share(place(chip, core, 0), left)
    share(place(chip, core, 0), sibling)
    share(place(chip, core, 1), sibling)

    for step in y_steps:
        other, where = y_peer(step)
        remote(ask, ask_y.at[other], ask_sy.at[step], ask_ry.at[other], where).wait_recv()
    for step in z_steps:
        other, where = z_peer(step)
        remote(ask, ask_z.at[other], ask_sz.at[step], ask_rz.at[other], where).wait_recv()
    to_scalars_y = pltpu.make_async_copy(ask_y, read_y, read_sem.at[0])
    to_scalars_z = pltpu.make_async_copy(ask_z, read_z, read_sem.at[1])
    to_scalars_y.start()
    to_scalars_z.start()
    to_scalars_y.wait()
    to_scalars_z.wait()

    for copy, peer in x_moves:
        remote(
            swap_out.at[peer], swap_in.at[peer], x_send.at[peer], x_recv.at[peer], {"narrow": peer}
        ).wait_recv()
    first = swap_in[block_list[0] // PER_DEV][0:rows, :]
    second = swap_in[block_list[1] // PER_DEV][rows : 2 * rows, :]
    hand0[...] = first
    hand1[...] = second
    got_z[at_z] = first
    got_y[at_y] = second
    for step in y_steps:
        other, where = y_peer(step)
        copy = remote(hand1, got_y.at[at_y], g_sy.at[step], g_ry.at[at_y], where)
        copy.start()
        sent.append(copy)
    for step in z_steps:
        other, where = z_peer(step)
        copy = remote(hand0, got_z.at[at_z], g_sz.at[step], g_rz.at[at_z], where)
        copy.start()
        sent.append(copy)

    def turn(b):
        base = pl.multiple_of(b * rows, rows)
        return mm_nt(res[pl.ds(base, rows), :], rot[block_list[b]]).astype(BF16)

    def from_y(source):
        return source // blocks // RING_Z

    def from_z(source):
        return source // blocks % RING_Z

    arrived(place(right_chip, core, 1))
    share(place(right_chip, core, 1), left)
    share(place(right_chip, core, 1), sibling)
    arrived(place(left_chip, core, 0))
    share(place(left_chip, core, 0), right)
    share(place(left_chip, core, 0), sibling)

    for step in y_steps:
        other, where = y_peer(step)
        remote(hand1, got_y.at[other], g_sy.at[step], g_ry.at[other], where).wait_recv()
    last_z[at_z] = got_y[from_y(sources[1])]
    for step in z_steps:
        other, where = z_peer(step)
        pass_z[other] = got_y[from_y(read_z[other, 1, 0])]
        copy = remote(pass_z.at[other], last_z.at[at_z], p_sz.at[step], p_rz.at[at_z], where)
        copy.start()
        sent.append(copy)

    arrived(place(right_chip, core, 0))
    share(place(right_chip, core, 0), sibling)
    arrived(place(left_chip, core, 1))
    share(place(left_chip, core, 1), sibling)

    for step in z_steps:
        other, where = z_peer(step)
        remote(hand0, got_z.at[other], g_sz.at[step], g_rz.at[other], where).wait_recv()
    last_y[at_y] = got_z[from_z(sources[0])]
    for step in y_steps:
        other, where = y_peer(step)
        pass_y[other] = got_z[from_z(read_y[other, 0, 0])]
        copy = remote(pass_y.at[other], last_y.at[at_y], p_sy.at[step], p_ry.at[at_y], where)
        copy.start()
        sent.append(copy)

    arrived(place(opposite, core, 1))
    share(place(opposite, core, 1), sibling)
    arrived(place(opposite, core, 0))
    share(place(opposite, core, 0), sibling)
    for owner_chip in (chip, left_chip, right_chip, opposite):
        for which in range(PER_DEV):
            arrived(place(owner_chip, 1 - core, which))

    def turn_one(b, carry):
        out[pl.ds(pl.multiple_of(b * rows, rows), rows), :] = turn(b)
        return carry

    lax.fori_loop(MOVE, blocks, turn_one, 0, unroll=2)

    for step in y_steps:
        other, where = y_peer(step)
        remote(hand1, last_y.at[other], p_sy.at[step], p_ry.at[other], where).wait_recv()
    out[0:rows, :] = last_y[from_y(sources[0])]
    for step in z_steps:
        other, where = z_peer(step)
        remote(hand0, last_z.at[other], p_sz.at[step], p_rz.at[other], where).wait_recv()
    out[rows : 2 * rows, :] = last_z[from_z(sources[1])]

    for copy in sent + raws + shares:
        copy.wait_send()


def local(points, targets, centroids, block_list, lengths, sources):
    blocks, rows, width = points.shape
    lists = centroids.shape[0]
    total = blocks * rows
    narrow_size = 2 * CHIPS_X
    hbm = pl.BlockSpec(memory_space=pltpu.HBM)
    dma = pltpu.SemaphoreType.DMA
    square = (width, width)
    tile = (rows, width)
    ask = (8, 128)
    rotated = pl.pallas_call(
        functools.partial(kernel, blocks, rows),
        out_shape=jax.ShapeDtypeStruct((total, width), BF16),
        in_specs=[hbm] * 6,
        out_specs=pl.BlockSpec(memory_space=pltpu.VMEM),
        scratch_shapes=[
            pltpu.VMEM(centroids.shape, F32),
            pltpu.SMEM((blocks,), jnp.int32),
            pltpu.SMEM((blocks,), jnp.int32),
            pltpu.SMEM((blocks,), jnp.int32),
            *[pltpu.VMEM((total, width), BF16)] * 6,
            pltpu.VMEM((width, 2 * total), BF16),
            pltpu.VMEM((4, *square), F32),
            pltpu.VMEM((6, *square), BF16),
            pltpu.VMEM((6, *square), BF16),
            pltpu.VMEM((narrow_size, MOVE * rows, width), BF16),
            pltpu.VMEM((MOVE, narrow_size * rows, width), BF16),
            pltpu.VMEM((PER_DEV, *square), F32),
            pltpu.VMEM((PER_DEV, *square), BF16),
            pltpu.VMEM((lists, *square), BF16),
            pltpu.VMEM((narrow_size, MOVE * rows, width), BF16),
            pltpu.VMEM((narrow_size, MOVE * rows, width), BF16),
            pltpu.VMEM(tile, BF16),
            pltpu.VMEM(tile, BF16),
            pltpu.VMEM((RING_Z, *tile), BF16),
            pltpu.VMEM((RING_Y, *tile), BF16),
            pltpu.VMEM((RING_Y, *tile), BF16),
            pltpu.VMEM((RING_Z, *tile), BF16),
            pltpu.VMEM((RING_Y, *tile), BF16),
            pltpu.VMEM((RING_Z, *tile), BF16),
            pltpu.VMEM(ask, jnp.int32),
            pltpu.VMEM((RING_Y, *ask), jnp.int32),
            pltpu.VMEM((RING_Z, *ask), jnp.int32),
            pltpu.SMEM((RING_Y, *ask), jnp.int32),
            pltpu.SMEM((RING_Z, *ask), jnp.int32),
            dma((6,)),
            dma((2,)),
            dma((2,)),
            dma((6,)),
            dma((narrow_size,)),
            dma((6,)),
            dma((6,)),
            dma((narrow_size,)),
            dma((narrow_size,)),
            dma((14,)),
            dma((lists,)),
            dma((RING_Y,)),
            dma((RING_Z,)),
            dma((RING_Y,)),
            dma((RING_Z,)),
            dma((RING_Z,)),
            dma((RING_Z,)),
            dma((RING_Y,)),
            dma((RING_Y,)),
            dma((RING_Y,)),
            dma((RING_Y,)),
            dma((RING_Z,)),
            dma((RING_Z,)),
            dma((2,)),
            pltpu.SemaphoreType.REGULAR((4,)),
        ],
        compiler_params=pltpu.CompilerParams(
            collective_id=0, has_side_effects=True, vmem_limit_bytes=60 << 20
        ),
        name="rotate_lists",
    )(
        points.reshape(total, width),
        targets.reshape(total, width),
        centroids,
        block_list,
        lengths,
        sources,
    )
    return rotated.reshape(blocks, rows, width)


def solution(mesh):
    return jax.shard_map(
        local,
        mesh=mesh,
        in_specs=(
            P("wide", "narrow", None),
            P("wide", "narrow", None),
            P("wide", None),
            P("wide"),
            P("wide"),
            P("wide"),
        ),
        out_specs=P("wide", "narrow", None),
        check_vma=False,
    )
```

```python
import functools

import jax
import jax.numpy as jnp
from jax import lax
from jax.experimental import pallas as pl
from jax.experimental.pallas import tpu as pltpu
from jax.sharding import PartitionSpec as P

MOVE = 2
SWEEPS = 5
CHIPS_X = 4
RING_Y = 8
RING_Z = 12
PER_DEV = 2

MESH = pl.DeviceIdType.MESH
BF16 = jnp.bfloat16
F32 = jnp.float32


def mm(a, b):
    return jnp.dot(a, b, preferred_element_type=F32)


def mm_nt(a, b):
    return lax.dot_general(a, b, (((1,), (1,)), ((), ())), preferred_element_type=F32)


def split_bf16(a):
    high = a.astype(BF16)
    return high, (a - high.astype(F32)).astype(BF16)


def remote(src, dst, send_sem, recv_sem, where):
    return pltpu.make_async_remote_copy(
        src_ref=src,
        dst_ref=dst,
        send_sem=send_sem,
        recv_sem=recv_sem,
        device_id=where,
        device_id_type=MESH,
    )


def x_partners(narrow):
    chip, core = narrow // 2, narrow % 2
    right = ((chip + 1) % CHIPS_X) * 2 + core
    left = ((chip + CHIPS_X - 1) % CHIPS_X) * 2 + core
    sibling = chip * 2 + 1 - core
    return chip, core, right, left, sibling


def kernel(
    blocks,
    rows,
    points,
    targets,
    centroids_hbm,
    block_list_hbm,
    lengths_hbm,
    sources_hbm,
    out,
    centroids,
    block_list,
    lengths,
    sources,
    own_p,
    own_t,
    sib_p,
    sib_t,
    res,
    res_sib,
    turned_t,
    kept,
    out_buf,
    in_buf,
    raw,
    hand_res,
    iterate,
    mine,
    rot,
    swap_out,
    swap_in0,
    swap_in1,
    hand0,
    hand1,
    got_z,
    got_y,
    pass_y,
    pass_z,
    last_y,
    last_z,
    ask,
    ask_y,
    ask_z,
    read_y,
    read_z,
    load_sem,
    swap_send,
    swap_recv,
    raw_send,
    raw_recv,
    gram_send,
    gram_recv,
    x_send,
    x_recv,
    rot_send,
    rot_recv,
    ask_sy,
    ask_sz,
    ask_ry,
    ask_rz,
    g_sz,
    g_rz,
    g_sy,
    g_ry,
    p_sy,
    p_ry,
    p_sz,
    p_rz,
    read_sem,
    near_sem,
):
    wide = lax.axis_index("wide")
    narrow = lax.axis_index("narrow")
    at_y, at_z = wide // RING_Z, wide % RING_Z
    chip, core, right, left, sibling = x_partners(narrow)
    right_chip = (chip + 1) % CHIPS_X
    left_chip = (chip + CHIPS_X - 1) % CHIPS_X
    opposite = (chip + 2) % CHIPS_X
    width = points.shape[1]
    total = blocks * rows
    handed = MOVE * rows

    def y_peer(step):
        other = (at_y + step) % RING_Y
        return other, {"wide": other * RING_Z + at_z}

    def z_peer(step):
        other = (at_z + step) % RING_Z
        return other, {"wide": at_y * RING_Z + other}

    y_steps = sorted(range(1, RING_Y), key=lambda s: -min(s, RING_Y - s))
    z_steps = sorted(range(1, RING_Z), key=lambda s: -min(s, RING_Z - s))
    around = (
        y_peer(1)[1],
        y_peer(RING_Y - 1)[1],
        z_peer(1)[1],
        z_peer(RING_Z - 1)[1],
    )

    barrier = pltpu.get_barrier_semaphore()
    for partner in (sibling, right, left):
        pl.semaphore_signal(barrier, inc=1, device_id={"narrow": partner}, device_id_type=MESH)
    for where in around:
        pl.semaphore_signal(barrier, inc=1, device_id=where, device_id_type=MESH)

    loads = [
        pltpu.make_async_copy(source, target, load_sem.at[index])
        for index, (source, target) in enumerate(
            (
                (targets, own_t),
                (points, own_p),
                (block_list_hbm, block_list),
                (lengths_hbm, lengths),
                (centroids_hbm, centroids),
                (sources_hbm, sources),
            )
        )
    ]
    for load in loads:
        load.start()
    pl.semaphore_wait(barrier, 3 + len(around))

    swap_t = remote(targets, sib_t, swap_send.at[0], swap_recv.at[0], {"narrow": sibling})
    swap_p = remote(points, sib_p, swap_send.at[1], swap_recv.at[1], {"narrow": sibling})
    swap_t.start()
    swap_p.start()
    sent = [swap_t, swap_p]

    raws = []

    def share_raw(src, owner, where):
        copy = remote(src, raw.at[owner], raw_send.at[len(raws)], raw_recv.at[owner], {"narrow": where})
        copy.start()
        raws.append(copy)

    def raw_arrived(owner):
        remote(
            raw.at[owner], raw.at[owner], raw_send.at[0], raw_recv.at[owner], {"narrow": sibling}
        ).wait_recv()

    share_raw(points.at[pl.ds(0, handed)], narrow, right)
    share_raw(points.at[pl.ds(0, handed)], narrow, left)

    def tell():
        for index, where in enumerate(around):
            pl.semaphore_signal(near_sem.at[index], inc=1, device_id=where, device_id_type=MESH)

    def tell_z():
        for index in (2, 3):
            pl.semaphore_signal(near_sem.at[index], inc=1, device_id=around[index], device_id_type=MESH)

    def hear(kinds):
        for index in kinds:
            pl.semaphore_wait(near_sem.at[index], 1)

    tell()

    def residual_of(value, block, first_row):
        centre = centroids[pl.ds(block_list[block], 1), :]
        row = first_row + lax.broadcasted_iota(jnp.int32, (rows, width), 0)
        return jnp.where(row < lengths[block], value.astype(F32) - centre, 0.0).astype(BF16)

    def residual_into(dst, src, first_row):
        def one(b, carry):
            here = pl.ds(pl.multiple_of(b * rows, rows), rows)
            dst[here, :] = residual_of(src[here, :], b, first_row)
            return carry

        lax.fori_loop(0, blocks, one, 0, unroll=4)

    def transpose_into(first, src):
        for piece in range(total // width):
            turned_t[:, first + piece * width : first + (piece + 1) * width] = src[
                piece * width : (piece + 1) * width, :
            ].T

    def half_gram(owner_chip, which, first, held):
        wanted = (owner_chip * 2 + core) * PER_DEV + which
        pieces = []
        for b in range(blocks):
            keep = jnp.where(block_list[b] == wanted, 1.0, 0.0).astype(BF16)
            pieces.append(held[b * rows : (b + 1) * rows, :] * keep)
        return mm(turned_t[:, first : first + total], jnp.concatenate(pieces, axis=0))

    def own_half(owner_chip, which):
        return half_gram(owner_chip, which, 0, res)

    def sib_half(owner_chip, which):
        return half_gram(owner_chip, which, total, res_sib)

    def hop(slot, where):
        return remote(
            out_buf.at[slot], in_buf.at[slot], gram_send.at[slot], gram_recv.at[slot], {"narrow": where}
        )

    hops = [hop(s, right if s % 2 == 0 else left) for s in range(6)]
    sent += hops
    early = ((opposite, 0), (opposite, 1), (right_chip, 1), (left_chip, 0))

    loads[0].wait()
    transpose_into(0, own_t)
    for load in loads[1:]:
        load.wait()
    residual_into(res, own_p, narrow * rows)
    for slot, (owner_chip, which) in enumerate(early):
        kept[slot] = own_half(owner_chip, which)
    swap_t.wait_recv()
    transpose_into(total, sib_t)
    swap_p.wait_recv()
    raw_arrived(left)
    share_raw(raw.at[left], left, right)
    residual_into(res_sib, sib_p, sibling * rows)

    def finish(slot):
        owner_chip, which = early[slot]
        out_buf[slot] = (kept[slot] + sib_half(owner_chip, which)).astype(BF16)
        hops[slot].start()

    finish(0)
    finish(1)
    hear((0, 1, 2, 3))
    tell()
    finish(2)
    share_raw(raw.at[left], left, sibling)
    raw_arrived(right)
    share_raw(raw.at[right], right, sibling)
    finish(3)
    hear((0, 1, 2, 3))
    tell()
    kept[0] = own_half(right_chip, 0) + sib_half(right_chip, 0)
    kept[1] = own_half(left_chip, 1) + sib_half(left_chip, 1)
    hops[0].wait_recv()
    out_buf[4] = (kept[0] + in_buf[0].astype(F32)).astype(BF16)
    hops[4].start()
    hops[1].wait_recv()
    out_buf[5] = (kept[1] + in_buf[1].astype(F32)).astype(BF16)
    hops[5].start()
    hear((0, 1, 2, 3))
    tell_z()
    across = opposite * 2 + core
    raw_arrived(across)
    share_raw(raw.at[across], across, sibling)
    kept[2] = own_half(chip, 0) + sib_half(chip, 0)
    hear((2, 3))
    tell_z()
    kept[3] = own_half(chip, 1) + sib_half(chip, 1)
    hear((2, 3))

    line = lax.broadcasted_iota(jnp.int32, ask.shape, 0)
    wish = jnp.where(line == 0, sources[0], sources[1])
    ask[...] = wish
    ask_y[at_y] = wish
    ask_z[at_z] = wish

    for step in y_steps:
        other, where = y_peer(step)
        copy = remote(ask, ask_y.at[at_y], ask_sy.at[step], ask_ry.at[at_y], where)
        copy.start()
        sent.append(copy)
    for step in z_steps:
        other, where = z_peer(step)
        copy = remote(ask, ask_z.at[at_z], ask_sz.at[step], ask_rz.at[at_z], where)
        copy.start()
        sent.append(copy)

    for b in range(MOVE):
        hand_res[b, pl.ds(pl.multiple_of(narrow * rows, rows), rows), :] = res[
            b * rows : (b + 1) * rows, :
        ]
        hand_res[b, pl.ds(pl.multiple_of(sibling * rows, rows), rows), :] = res_sib[
            b * rows : (b + 1) * rows, :
        ]
    for owner_chip in (left_chip, right_chip, opposite):
        raw_arrived(owner_chip * 2 + 1 - core)
        for owner_core in range(2):
            owner = owner_chip * 2 + owner_core
            for b in range(MOVE):
                hand_res[b, pl.ds(pl.multiple_of(owner * rows, rows), rows), :] = residual_of(
                    raw[owner, b * rows : (b + 1) * rows, :], b, owner * rows
                )

    hops[3].wait_recv()
    kept[2] = kept[2] + in_buf[3].astype(F32)
    hops[2].wait_recv()
    kept[3] = kept[3] + in_buf[2].astype(F32)
    hops[4].wait_recv()
    hops[5].wait_recv()
    for which in range(PER_DEV):
        total_gram = kept[2 + which] + in_buf[4 + which].astype(F32)
        norm = jnp.sqrt(jnp.sum(total_gram * total_gram, keepdims=True) + 1e-06)
        iterate[which] = total_gram / norm

    def sweep(index, carry):
        for which in range(PER_DEV):
            held = iterate[which].astype(BF16)
            product = mm_nt(held, held).astype(BF16)
            iterate[which] = 1.5 * iterate[which] - 0.5 * mm(product, held)
        return carry

    lax.fori_loop(0, SWEEPS - 1, sweep, 0)
    for which in range(PER_DEV):
        exact = iterate[which]
        high, low = split_bf16(exact)
        product = mm_nt(high, high) + (mm_nt(high, low) + mm_nt(low, high))
        p_high, p_low = split_bf16(product)
        cubed = mm(p_high, high) + (mm(p_high, low) + mm(p_low, high))
        rotation = (1.5 * exact - 0.5 * cubed).astype(BF16)
        mine[which] = rotation
        rot[narrow * PER_DEV + which] = rotation

    swap_in = (swap_in0, swap_in1)
    x_peers = []
    for chip_step, flip in ((2, 0), (2, 1), (1, 0), (1, 1), (3, 0), (3, 1), (0, 1)):
        peer_core = core + flip - 2 * core * flip
        x_peers.append(((chip + chip_step) % CHIPS_X) * 2 + peer_core)
    for b in range(MOVE):
        chosen = mine[block_list[b] % PER_DEV]
        swap_out[b] = mm_nt(hand_res[b], chosen).astype(BF16).reshape(2 * CHIPS_X, rows, width)
        swap_in[b][narrow] = swap_out[b, narrow]
        for peer in x_peers:
            copy = remote(
                swap_out.at[b, peer],
                swap_in[b].at[narrow],
                x_send.at[b, peer],
                x_recv.at[b, narrow],
                {"narrow": peer},
            )
            copy.start()
            sent.append(copy)

    def x_arrived(b):
        for peer in x_peers:
            remote(
                swap_out.at[b, peer], swap_in[b].at[peer], x_send.at[b, peer], x_recv.at[b, peer], {"narrow": peer}
            ).wait_recv()

    def place(owner_chip, owner_core, which):
        return (owner_chip * 2 + owner_core) * PER_DEV + which

    shares = []

    def share(slot, where):
        copy = remote(
            rot.at[slot], rot.at[slot], rot_send.at[len(shares)], rot_recv.at[slot], {"narrow": where}
        )
        copy.start()
        shares.append(copy)

    def arrived(slot):
        remote(rot.at[slot], rot.at[slot], rot_send.at[0], rot_recv.at[slot], {"narrow": sibling}).wait_recv()

    share(place(chip, core, 1), left)
    share(place(chip, core, 0), left)
    share(place(chip, core, 0), sibling)
    share(place(chip, core, 1), sibling)

    for step in y_steps:
        other, where = y_peer(step)
        remote(ask, ask_y.at[other], ask_sy.at[step], ask_ry.at[other], where).wait_recv()
    for step in z_steps:
        other, where = z_peer(step)
        remote(ask, ask_z.at[other], ask_sz.at[step], ask_rz.at[other], where).wait_recv()
    to_scalars_y = pltpu.make_async_copy(ask_y, read_y, read_sem.at[0])
    to_scalars_z = pltpu.make_async_copy(ask_z, read_z, read_sem.at[1])
    to_scalars_y.start()
    to_scalars_z.start()
    to_scalars_y.wait()
    to_scalars_z.wait()

    x_arrived(0)
    first = swap_in0[block_list[0] // PER_DEV]
    hand0[...] = first
    got_z[at_z] = first
    for step in z_steps:
        other, where = z_peer(step)
        copy = remote(hand0, got_z.at[at_z], g_sz.at[step], g_rz.at[at_z], where)
        copy.start()
        sent.append(copy)
    share(place(chip, core, 0), right)
    share(place(chip, core, 1), right)
    x_arrived(1)
    second = swap_in1[block_list[1] // PER_DEV]
    hand1[...] = second
    got_y[at_y] = second
    for step in y_steps:
        other, where = y_peer(step)
        copy = remote(hand1, got_y.at[at_y], g_sy.at[step], g_ry.at[at_y], where)
        copy.start()
        sent.append(copy)

    def turn(b):
        base = pl.multiple_of(b * rows, rows)
        return mm_nt(res[pl.ds(base, rows), :], rot[block_list[b]]).astype(BF16)

    def from_y(source):
        return source // blocks // RING_Z

    def from_z(source):
        return source // blocks % RING_Z

    for step in y_steps:
        other, where = y_peer(step)
        remote(hand1, got_y.at[other], g_sy.at[step], g_ry.at[other], where).wait_recv()
    last_z[at_z] = got_y[from_y(sources[1])]
    for step in z_steps:
        other, where = z_peer(step)
        pass_z[other] = got_y[from_y(read_z[other, 1, 0])]
        copy = remote(pass_z.at[other], last_z.at[at_z], p_sz.at[step], p_rz.at[at_z], where)
        copy.start()
        sent.append(copy)

    arrived(place(right_chip, core, 1))
    share(place(right_chip, core, 1), left)
    share(place(right_chip, core, 1), sibling)
    arrived(place(left_chip, core, 0))
    share(place(left_chip, core, 0), right)
    share(place(left_chip, core, 0), sibling)

    for step in z_steps:
        other, where = z_peer(step)
        remote(hand0, got_z.at[other], g_sz.at[step], g_rz.at[other], where).wait_recv()
    last_y[at_y] = got_z[from_z(sources[0])]
    for step in y_steps:
        other, where = y_peer(step)
        pass_y[other] = got_z[from_z(read_y[other, 0, 0])]
        copy = remote(pass_y.at[other], last_y.at[at_y], p_sy.at[step], p_ry.at[at_y], where)
        copy.start()
        sent.append(copy)

    arrived(place(right_chip, core, 0))
    share(place(right_chip, core, 0), sibling)
    arrived(place(left_chip, core, 1))
    share(place(left_chip, core, 1), sibling)
    arrived(place(opposite, core, 1))
    share(place(opposite, core, 1), sibling)
    arrived(place(opposite, core, 0))
    share(place(opposite, core, 0), sibling)
    for owner_chip in (chip, left_chip, right_chip, opposite):
        for which in range(PER_DEV):
            arrived(place(owner_chip, 1 - core, which))

    def turn_one(b, carry):
        out[pl.ds(pl.multiple_of(b * rows, rows), rows), :] = turn(b)
        return carry

    lax.fori_loop(MOVE, blocks, turn_one, 0, unroll=2)

    for step in y_steps:
        other, where = y_peer(step)
        remote(hand1, last_y.at[other], p_sy.at[step], p_ry.at[other], where).wait_recv()
    out[0:rows, :] = last_y[from_y(sources[0])]
    for step in z_steps:
        other, where = z_peer(step)
        remote(hand0, last_z.at[other], p_sz.at[step], p_rz.at[other], where).wait_recv()
    out[rows : 2 * rows, :] = last_z[from_z(sources[1])]

    for copy in sent + raws + shares:
        copy.wait_send()


def local(points, targets, centroids, block_list, lengths, sources):
    blocks, rows, width = points.shape
    lists = centroids.shape[0]
    total = blocks * rows
    narrow_size = 2 * CHIPS_X
    hbm = pl.BlockSpec(memory_space=pltpu.HBM)
    dma = pltpu.SemaphoreType.DMA
    square = (width, width)
    tile = (rows, width)
    ask = (8, 128)
    rotated = pl.pallas_call(
        functools.partial(kernel, blocks, rows),
        out_shape=pltpu.VMEM((total, width), BF16),
        in_specs=[hbm] * 6,
        out_specs=pl.BlockSpec(memory_space=pltpu.VMEM),
        scratch_shapes=[
            pltpu.VMEM(centroids.shape, F32),
            pltpu.SMEM((blocks,), jnp.int32),
            pltpu.SMEM((blocks,), jnp.int32),
            pltpu.SMEM((blocks,), jnp.int32),
            *[pltpu.VMEM((total, width), BF16)] * 6,
            pltpu.VMEM((width, 2 * total), BF16),
            pltpu.VMEM((4, *square), F32),
            pltpu.VMEM((6, *square), BF16),
            pltpu.VMEM((6, *square), BF16),
            pltpu.VMEM((narrow_size, MOVE * rows, width), BF16),
            pltpu.VMEM((MOVE, narrow_size * rows, width), BF16),
            pltpu.VMEM((PER_DEV, *square), F32),
            pltpu.VMEM((PER_DEV, *square), BF16),
            pltpu.VMEM((lists, *square), BF16),
            pltpu.VMEM((MOVE, narrow_size, rows, width), BF16),
            pltpu.VMEM((narrow_size, rows, width), BF16),
            pltpu.VMEM((narrow_size, rows, width), BF16),
            pltpu.VMEM(tile, BF16),
            pltpu.VMEM(tile, BF16),
            pltpu.VMEM((RING_Z, *tile), BF16),
            pltpu.VMEM((RING_Y, *tile), BF16),
            pltpu.VMEM((RING_Y, *tile), BF16),
            pltpu.VMEM((RING_Z, *tile), BF16),
            pltpu.VMEM((RING_Y, *tile), BF16),
            pltpu.VMEM((RING_Z, *tile), BF16),
            pltpu.VMEM(ask, jnp.int32),
            pltpu.VMEM((RING_Y, *ask), jnp.int32),
            pltpu.VMEM((RING_Z, *ask), jnp.int32),
            pltpu.SMEM((RING_Y, *ask), jnp.int32),
            pltpu.SMEM((RING_Z, *ask), jnp.int32),
            dma((6,)),
            dma((2,)),
            dma((2,)),
            dma((6,)),
            dma((narrow_size,)),
            dma((6,)),
            dma((6,)),
            dma((MOVE, narrow_size)),
            dma((MOVE, narrow_size)),
            dma((14,)),
            dma((lists,)),
            dma((RING_Y,)),
            dma((RING_Z,)),
            dma((RING_Y,)),
            dma((RING_Z,)),
            dma((RING_Z,)),
            dma((RING_Z,)),
            dma((RING_Y,)),
            dma((RING_Y,)),
            dma((RING_Y,)),
            dma((RING_Y,)),
            dma((RING_Z,)),
            dma((RING_Z,)),
            dma((2,)),
            pltpu.SemaphoreType.REGULAR((4,)),
        ],
        compiler_params=pltpu.CompilerParams(
            collective_id=0, has_side_effects=True, vmem_limit_bytes=60 << 20
        ),
        name="rotate_lists",
    )(
        points.reshape(total, width),
        targets.reshape(total, width),
        centroids,
        block_list,
        lengths,
        sources,
    )
    return rotated.reshape(blocks, rows, width)


def solution(mesh):
    return jax.shard_map(
        local,
        mesh=mesh,
        in_specs=(
            P("wide", "narrow", None),
            P("wide", "narrow", None),
            P("wide", None),
            P("wide"),
            P("wide"),
            P("wide"),
        ),
        out_specs=P("wide", "narrow", None),
        check_vma=False,
    )
```

```python
import functools

import jax
import jax.numpy as jnp
from jax import lax
from jax.experimental import pallas as pl
from jax.experimental.pallas import tpu as pltpu
from jax.sharding import PartitionSpec as P

MOVE = 2
SWEEPS = 5
CHIPS_X = 4
RING_Y = 8
RING_Z = 12
PER_DEV = 2
REACH = 3

MESH = pl.DeviceIdType.MESH
BF16 = jnp.bfloat16
F32 = jnp.float32


def mm(a, b):
    return jnp.dot(a, b, preferred_element_type=F32)


def mm_nt(a, b):
    return lax.dot_general(a, b, (((1,), (1,)), ((), ())), preferred_element_type=F32)


def split_bf16(a):
    high = a.astype(BF16)
    return high, (a - high.astype(F32)).astype(BF16)


def remote(src, dst, send_sem, recv_sem, where):
    return pltpu.make_async_remote_copy(
        src_ref=src,
        dst_ref=dst,
        send_sem=send_sem,
        recv_sem=recv_sem,
        device_id=where,
        device_id_type=MESH,
    )


def x_partners(narrow):
    chip, core = narrow // 2, narrow % 2
    right = ((chip + 1) % CHIPS_X) * 2 + core
    left = ((chip + CHIPS_X - 1) % CHIPS_X) * 2 + core
    sibling = chip * 2 + 1 - core
    return chip, core, right, left, sibling


def kernel(
    blocks,
    rows,
    points,
    targets,
    centroids_hbm,
    block_list_hbm,
    lengths_hbm,
    sources_hbm,
    out,
    centroids,
    block_list,
    lengths,
    sources,
    own_p,
    own_t,
    sib_p,
    sib_t,
    res,
    res_sib,
    turned_t,
    kept,
    out_buf,
    in_buf,
    raw,
    hand_res,
    iterate,
    mine,
    rot,
    swap_out,
    swap_in0,
    swap_in1,
    hand0,
    hand1,
    got_z,
    got_y,
    pass_y,
    pass_z,
    last_y,
    last_z,
    ask,
    ask_y,
    ask_z,
    read_y,
    read_z,
    load_sem,
    swap_send,
    swap_recv,
    raw_send,
    raw_recv,
    gram_send,
    gram_recv,
    x_send,
    x_recv,
    rot_send,
    rot_recv,
    ask_sy,
    ask_sz,
    ask_ry,
    ask_rz,
    g_sz,
    g_rz,
    g_sy,
    g_ry,
    p_sy,
    p_ry,
    p_sz,
    p_rz,
    read_sem,
    near_sem,
):
    wide = lax.axis_index("wide")
    narrow = lax.axis_index("narrow")
    at_y, at_z = wide // RING_Z, wide % RING_Z
    chip, core, right, left, sibling = x_partners(narrow)
    right_chip = (chip + 1) % CHIPS_X
    left_chip = (chip + CHIPS_X - 1) % CHIPS_X
    opposite = (chip + 2) % CHIPS_X
    width = points.shape[1]
    total = blocks * rows
    handed = MOVE * rows

    def y_peer(step):
        other = (at_y + step) % RING_Y
        return other, {"wide": other * RING_Z + at_z}

    def z_peer(step):
        other = (at_z + step) % RING_Z
        return other, {"wide": at_y * RING_Z + other}

    y_steps = sorted(range(1, RING_Y), key=lambda s: -min(s, RING_Y - s))
    z_steps = sorted(range(1, RING_Z), key=lambda s: -min(s, RING_Z - s))
    around = (
        y_peer(1)[1],
        y_peer(RING_Y - 1)[1],
        z_peer(1)[1],
        z_peer(RING_Z - 1)[1],
    )

    barrier = pltpu.get_barrier_semaphore()
    for partner in (sibling, right, left):
        pl.semaphore_signal(barrier, inc=1, device_id={"narrow": partner}, device_id_type=MESH)
    for where in around:
        pl.semaphore_signal(barrier, inc=1, device_id=where, device_id_type=MESH)

    loads = [
        pltpu.make_async_copy(source, target, load_sem.at[index])
        for index, (source, target) in enumerate(
            (
                (targets, own_t),
                (points, own_p),
                (block_list_hbm, block_list),
                (lengths_hbm, lengths),
                (centroids_hbm, centroids),
                (sources_hbm, sources),
            )
        )
    ]
    for load in loads:
        load.start()
    pl.semaphore_wait(barrier, 3 + len(around))

    swap_t = remote(targets, sib_t, swap_send.at[0], swap_recv.at[0], {"narrow": sibling})
    swap_p = remote(points, sib_p, swap_send.at[1], swap_recv.at[1], {"narrow": sibling})
    swap_t.start()
    swap_p.start()
    sent = [swap_t, swap_p]

    raws = []

    def share_raw(src, owner, where):
        copy = remote(src, raw.at[owner], raw_send.at[len(raws)], raw_recv.at[owner], {"narrow": where})
        copy.start()
        raws.append(copy)

    def raw_arrived(owner):
        remote(
            raw.at[owner], raw.at[owner], raw_send.at[0], raw_recv.at[owner], {"narrow": sibling}
        ).wait_recv()

    share_raw(points.at[pl.ds(0, handed)], narrow, right)
    share_raw(points.at[pl.ds(0, handed)], narrow, left)

    def tell():
        for index, where in enumerate(around):
            pl.semaphore_signal(near_sem.at[index], inc=1, device_id=where, device_id_type=MESH)

    def tell_z():
        for index in (2, 3):
            pl.semaphore_signal(near_sem.at[index], inc=1, device_id=around[index], device_id_type=MESH)

    def hear(kinds):
        for index in kinds:
            pl.semaphore_wait(near_sem.at[index], 1)

    tell()

    def residual_of(value, block, first_row):
        centre = centroids[pl.ds(block_list[block], 1), :]
        row = first_row + lax.broadcasted_iota(jnp.int32, (rows, width), 0)
        return jnp.where(row < lengths[block], value.astype(F32) - centre, 0.0).astype(BF16)

    def residual_into(dst, src, first_row):
        def one(b, carry):
            here = pl.ds(pl.multiple_of(b * rows, rows), rows)
            dst[here, :] = residual_of(src[here, :], b, first_row)
            return carry

        lax.fori_loop(0, blocks, one, 0, unroll=4)

    def transpose_into(first, src):
        for piece in range(total // width):
            turned_t[:, first + piece * width : first + (piece + 1) * width] = src[
                piece * width : (piece + 1) * width, :
            ].T

    def half_gram(owner_chip, which, first, held):
        wanted = (owner_chip * 2 + core) * PER_DEV + which
        pieces = []
        for b in range(blocks):
            keep = jnp.where(block_list[b] == wanted, 1.0, 0.0).astype(BF16)
            pieces.append(held[b * rows : (b + 1) * rows, :] * keep)
        return mm(turned_t[:, first : first + total], jnp.concatenate(pieces, axis=0))

    def own_half(owner_chip, which):
        return half_gram(owner_chip, which, 0, res)

    def sib_half(owner_chip, which):
        return half_gram(owner_chip, which, total, res_sib)

    def hop(slot, where):
        return remote(
            out_buf.at[slot], in_buf.at[slot], gram_send.at[slot], gram_recv.at[slot], {"narrow": where}
        )

    hops = [hop(s, right if s % 2 == 0 else left) for s in range(6)]
    sent += hops
    early = ((opposite, 0), (opposite, 1), (right_chip, 1), (left_chip, 0))

    loads[0].wait()
    transpose_into(0, own_t)
    for load in loads[1:]:
        load.wait()
    residual_into(res, own_p, narrow * rows)
    for slot, (owner_chip, which) in enumerate(early):
        kept[slot] = own_half(owner_chip, which)
    swap_t.wait_recv()
    transpose_into(total, sib_t)
    swap_p.wait_recv()
    raw_arrived(left)
    share_raw(raw.at[left], left, right)
    residual_into(res_sib, sib_p, sibling * rows)

    def finish(slot):
        owner_chip, which = early[slot]
        out_buf[slot] = (kept[slot] + sib_half(owner_chip, which)).astype(BF16)
        hops[slot].start()

    finish(0)
    finish(1)
    hear((0, 1, 2, 3))
    tell()
    finish(2)
    share_raw(raw.at[left], left, sibling)
    raw_arrived(right)
    share_raw(raw.at[right], right, sibling)
    finish(3)
    hear((0, 1, 2, 3))
    tell()
    kept[0] = own_half(right_chip, 0) + sib_half(right_chip, 0)
    kept[1] = own_half(left_chip, 1) + sib_half(left_chip, 1)
    hops[0].wait_recv()
    out_buf[4] = (kept[0] + in_buf[0].astype(F32)).astype(BF16)
    hops[4].start()
    hops[1].wait_recv()
    out_buf[5] = (kept[1] + in_buf[1].astype(F32)).astype(BF16)
    hops[5].start()
    hear((0, 1, 2, 3))
    tell_z()
    across = opposite * 2 + core
    raw_arrived(across)
    share_raw(raw.at[across], across, sibling)
    kept[2] = own_half(chip, 0) + sib_half(chip, 0)
    hear((2, 3))
    tell_z()
    kept[3] = own_half(chip, 1) + sib_half(chip, 1)
    hear((2, 3))

    line = lax.broadcasted_iota(jnp.int32, ask.shape, 0)
    wish = jnp.where(line == 0, sources[0], sources[1])
    ask[...] = wish
    ask_y[at_y] = wish
    ask_z[at_z] = wish

    for step in y_steps:
        other, where = y_peer(step)
        copy = remote(ask, ask_y.at[at_y], ask_sy.at[step], ask_ry.at[at_y], where)
        copy.start()
        sent.append(copy)
    for step in z_steps:
        other, where = z_peer(step)
        copy = remote(ask, ask_z.at[at_z], ask_sz.at[step], ask_rz.at[at_z], where)
        copy.start()
        sent.append(copy)

    for b in range(MOVE):
        hand_res[b, pl.ds(pl.multiple_of(narrow * rows, rows), rows), :] = res[
            b * rows : (b + 1) * rows, :
        ]
        hand_res[b, pl.ds(pl.multiple_of(sibling * rows, rows), rows), :] = res_sib[
            b * rows : (b + 1) * rows, :
        ]
    for owner_chip in (left_chip, right_chip, opposite):
        raw_arrived(owner_chip * 2 + 1 - core)
        for owner_core in range(2):
            owner = owner_chip * 2 + owner_core
            for b in range(MOVE):
                hand_res[b, pl.ds(pl.multiple_of(owner * rows, rows), rows), :] = residual_of(
                    raw[owner, b * rows : (b + 1) * rows, :], b, owner * rows
                )

    hops[3].wait_recv()
    kept[2] = kept[2] + in_buf[3].astype(F32)
    hops[2].wait_recv()
    kept[3] = kept[3] + in_buf[2].astype(F32)
    hops[4].wait_recv()
    hops[5].wait_recv()
    for which in range(PER_DEV):
        total_gram = kept[2 + which] + in_buf[4 + which].astype(F32)
        norm = jnp.sqrt(jnp.sum(total_gram * total_gram, keepdims=True) + 1e-06)
        iterate[which] = total_gram / norm

    def sweep(index, carry):
        for which in range(PER_DEV):
            held = iterate[which].astype(BF16)
            product = mm_nt(held, held).astype(BF16)
            iterate[which] = 1.5 * iterate[which] - 0.5 * mm(product, held)
        return carry

    lax.fori_loop(0, SWEEPS - 1, sweep, 0)
    for which in range(PER_DEV):
        exact = iterate[which]
        high, low = split_bf16(exact)
        product = mm_nt(high, high) + (mm_nt(high, low) + mm_nt(low, high))
        p_high, p_low = split_bf16(product)
        cubed = mm(p_high, high) + (mm(p_high, low) + mm(p_low, high))
        rotation = (1.5 * exact - 0.5 * cubed).astype(BF16)
        mine[which] = rotation
        rot[narrow * PER_DEV + which] = rotation

    swap_in = (swap_in0, swap_in1)
    x_peers = []
    for chip_step, flip in ((2, 0), (2, 1), (1, 0), (1, 1), (3, 0), (3, 1), (0, 1)):
        peer_core = core + flip - 2 * core * flip
        x_peers.append(((chip + chip_step) % CHIPS_X) * 2 + peer_core)
    for b in reversed(range(MOVE)):
        chosen = mine[block_list[b] % PER_DEV]
        swap_out[b] = mm_nt(hand_res[b], chosen).astype(BF16).reshape(2 * CHIPS_X, rows, width)
        swap_in[b][narrow] = swap_out[b, narrow]
        for peer in x_peers:
            copy = remote(
                swap_out.at[b, peer],
                swap_in[b].at[narrow],
                x_send.at[b, peer],
                x_recv.at[b, narrow],
                {"narrow": peer},
            )
            copy.start()
            sent.append(copy)

    def x_arrived(b):
        for peer in x_peers:
            remote(
                swap_out.at[b, peer], swap_in[b].at[peer], x_send.at[b, peer], x_recv.at[b, peer], {"narrow": peer}
            ).wait_recv()

    def place(owner_chip, owner_core, which):
        return (owner_chip * 2 + owner_core) * PER_DEV + which

    shares = []

    def share(slot, where):
        copy = remote(
            rot.at[slot], rot.at[slot], rot_send.at[len(shares)], rot_recv.at[slot], {"narrow": where}
        )
        copy.start()
        shares.append(copy)

    def arrived(slot):
        remote(rot.at[slot], rot.at[slot], rot_send.at[0], rot_recv.at[slot], {"narrow": sibling}).wait_recv()

    share(place(chip, core, 1), left)
    share(place(chip, core, 0), left)
    share(place(chip, core, 0), sibling)
    share(place(chip, core, 1), sibling)

    for step in y_steps:
        other, where = y_peer(step)
        remote(ask, ask_y.at[other], ask_sy.at[step], ask_ry.at[other], where).wait_recv()
    for step in z_steps:
        other, where = z_peer(step)
        remote(ask, ask_z.at[other], ask_sz.at[step], ask_rz.at[other], where).wait_recv()
    to_scalars_y = pltpu.make_async_copy(ask_y, read_y, read_sem.at[0])
    to_scalars_z = pltpu.make_async_copy(ask_z, read_z, read_sem.at[1])
    to_scalars_y.start()
    to_scalars_z.start()
    to_scalars_y.wait()
    to_scalars_z.wait()

    x_arrived(1)
    second = swap_in1[block_list[1] // PER_DEV]
    hand1[...] = second
    got_y[at_y] = second
    for step in y_steps:
        other, where = y_peer(step)
        copy = remote(hand1, got_y.at[at_y], g_sy.at[step], g_ry.at[at_y], where)
        copy.start()
        sent.append(copy)
    share(place(chip, core, 0), right)
    share(place(chip, core, 1), right)
    x_arrived(0)
    first = swap_in0[block_list[0] // PER_DEV]
    hand0[...] = first
    got_z[at_z] = first
    for step in (REACH, RING_Z - REACH, 2, RING_Z - 2, 1, RING_Z - 1):
        other, where = z_peer(step)
        copy = remote(hand0, got_z.at[at_z], g_sz.at[step], g_rz.at[at_z], where)
        copy.start()
        sent.append(copy)

    def z_arrived(step):
        other, where = z_peer(step)
        remote(hand0, got_z.at[other], g_sz.at[step], g_rz.at[other], where).wait_recv()

    def z_relay(source_step, onward, index):
        source, where = z_peer(source_step)
        copy = remote(
            got_z.at[source], got_z.at[source], g_sz.at[index], g_rz.at[source], z_peer(onward)[1]
        )
        copy.start()
        sent.append(copy)

    def share_if(here, slot, where, index):
        copy = remote(
            rot.at[slot], rot.at[slot], rot_send.at[index], rot_recv.at[slot], {"narrow": where}
        )

        @pl.when(here)
        def _():
            copy.start()

        return copy

    arrived(place(right_chip, core, 1))
    share(place(right_chip, core, 1), left)
    share(place(right_chip, core, 1), sibling)

    z_arrived(RING_Z - REACH)
    z_relay(RING_Z - REACH, 3, 6)
    z_relay(RING_Z - REACH, 2, 5)
    z_relay(RING_Z - REACH, 1, 4)
    z_arrived(REACH)
    z_relay(REACH, RING_Z - 2, 7)
    z_relay(REACH, RING_Z - 1, 8)

    arrived(place(left_chip, core, 0))
    share_if(core == 0, place(left_chip, core, 0), right, 14)
    share(place(left_chip, core, 0), sibling)

    def turn(b):
        base = pl.multiple_of(b * rows, rows)
        return mm_nt(res[pl.ds(base, rows), :], rot[block_list[b]]).astype(BF16)

    def from_y(source):
        return source // blocks // RING_Z

    def from_z(source):
        return source // blocks % RING_Z

    for step in y_steps:
        other, where = y_peer(step)
        remote(hand1, got_y.at[other], g_sy.at[step], g_ry.at[other], where).wait_recv()
    last_z[at_z] = got_y[from_y(sources[1])]
    for step in z_steps:
        other, where = z_peer(step)
        pass_z[other] = got_y[from_y(read_z[other, 1, 0])]
        copy = remote(pass_z.at[other], last_z.at[at_z], p_sz.at[step], p_rz.at[at_z], where)
        copy.start()
        sent.append(copy)

    arrived(place(right_chip, core, 0))
    odd_relay = share_if(core == 1, place(right_chip, core, 0), left, 14)
    share(place(right_chip, core, 0), sibling)
    arrived(place(left_chip, core, 1))
    share(place(left_chip, core, 1), sibling)

    for step in z_steps:
        if step not in (REACH, RING_Z - REACH):
            z_arrived(step)
    last_y[at_y] = got_z[from_z(sources[0])]
    for step in y_steps:
        other, where = y_peer(step)
        pass_y[other] = got_z[from_z(read_y[other, 0, 0])]
        copy = remote(pass_y.at[other], last_y.at[at_y], p_sy.at[step], p_ry.at[at_y], where)
        copy.start()
        sent.append(copy)

    arrived(place(opposite, core, 1))
    share(place(opposite, core, 1), sibling)
    arrived(place(opposite, core, 0))
    share(place(opposite, core, 0), sibling)
    for owner_chip in (chip, left_chip, right_chip, opposite):
        for which in range(PER_DEV):
            arrived(place(owner_chip, 1 - core, which))

    def turn_one(b, carry):
        out[pl.ds(pl.multiple_of(b * rows, rows), rows), :] = turn(b)
        return carry

    lax.fori_loop(MOVE, blocks, turn_one, 0, unroll=6)

    for step in y_steps:
        other, where = y_peer(step)
        remote(hand1, last_y.at[other], p_sy.at[step], p_ry.at[other], where).wait_recv()
    out[0:rows, :] = last_y[from_y(sources[0])]
    for step in z_steps:
        other, where = z_peer(step)
        remote(hand0, last_z.at[other], p_sz.at[step], p_rz.at[other], where).wait_recv()
    out[rows : 2 * rows, :] = last_z[from_z(sources[1])]

    for copy in sent + raws + shares + [odd_relay]:
        copy.wait_send()


def local(points, targets, centroids, block_list, lengths, sources):
    blocks, rows, width = points.shape
    lists = centroids.shape[0]
    total = blocks * rows
    narrow_size = 2 * CHIPS_X
    hbm = pl.BlockSpec(memory_space=pltpu.HBM)
    dma = pltpu.SemaphoreType.DMA
    square = (width, width)
    tile = (rows, width)
    ask = (8, 128)
    rotated = pl.pallas_call(
        functools.partial(kernel, blocks, rows),
        out_shape=pltpu.VMEM((total, width), BF16),
        in_specs=[hbm] * 6,
        out_specs=pl.BlockSpec(memory_space=pltpu.VMEM),
        scratch_shapes=[
            pltpu.VMEM(centroids.shape, F32),
            pltpu.SMEM((blocks,), jnp.int32),
            pltpu.SMEM((blocks,), jnp.int32),
            pltpu.SMEM((blocks,), jnp.int32),
            *[pltpu.VMEM((total, width), BF16)] * 6,
            pltpu.VMEM((width, 2 * total), BF16),
            pltpu.VMEM((4, *square), F32),
            pltpu.VMEM((6, *square), BF16),
            pltpu.VMEM((6, *square), BF16),
            pltpu.VMEM((narrow_size, MOVE * rows, width), BF16),
            pltpu.VMEM((MOVE, narrow_size * rows, width), BF16),
            pltpu.VMEM((PER_DEV, *square), F32),
            pltpu.VMEM((PER_DEV, *square), BF16),
            pltpu.VMEM((lists, *square), BF16),
            pltpu.VMEM((MOVE, narrow_size, rows, width), BF16),
            pltpu.VMEM((narrow_size, rows, width), BF16),
            pltpu.VMEM((narrow_size, rows, width), BF16),
            pltpu.VMEM(tile, BF16),
            pltpu.VMEM(tile, BF16),
            pltpu.VMEM((RING_Z, *tile), BF16),
            pltpu.VMEM((RING_Y, *tile), BF16),
            pltpu.VMEM((RING_Y, *tile), BF16),
            pltpu.VMEM((RING_Z, *tile), BF16),
            pltpu.VMEM((RING_Y, *tile), BF16),
            pltpu.VMEM((RING_Z, *tile), BF16),
            pltpu.VMEM(ask, jnp.int32),
            pltpu.VMEM((RING_Y, *ask), jnp.int32),
            pltpu.VMEM((RING_Z, *ask), jnp.int32),
            pltpu.SMEM((RING_Y, *ask), jnp.int32),
            pltpu.SMEM((RING_Z, *ask), jnp.int32),
            dma((6,)),
            dma((2,)),
            dma((2,)),
            dma((6,)),
            dma((narrow_size,)),
            dma((6,)),
            dma((6,)),
            dma((MOVE, narrow_size)),
            dma((MOVE, narrow_size)),
            dma((15,)),
            dma((lists,)),
            dma((RING_Y,)),
            dma((RING_Z,)),
            dma((RING_Y,)),
            dma((RING_Z,)),
            dma((RING_Z,)),
            dma((RING_Z,)),
            dma((RING_Y,)),
            dma((RING_Y,)),
            dma((RING_Y,)),
            dma((RING_Y,)),
            dma((RING_Z,)),
            dma((RING_Z,)),
            dma((2,)),
            pltpu.SemaphoreType.REGULAR((4,)),
        ],
        compiler_params=pltpu.CompilerParams(
            collective_id=0, has_side_effects=True, vmem_limit_bytes=60 << 20
        ),
        name="rotate_lists",
    )(
        points.reshape(total, width),
        targets.reshape(total, width),
        centroids,
        block_list,
        lengths,
        sources,
    )
    return rotated.reshape(blocks, rows, width)


def solution(mesh):
    return jax.shard_map(
        local,
        mesh=mesh,
        in_specs=(
            P("wide", "narrow", None),
            P("wide", "narrow", None),
            P("wide", None),
            P("wide"),
            P("wide"),
            P("wide"),
        ),
        out_specs=P("wide", "narrow", None),
        check_vma=False,
    )
```

```python
import functools

import jax
import jax.numpy as jnp
from jax import lax
from jax.experimental import pallas as pl
from jax.experimental.pallas import tpu as pltpu
from jax.sharding import PartitionSpec as P

MOVE = 2
SWEEPS = 5
CHIPS_X = 4
RING_Y = 8
RING_Z = 12
PER_DEV = 2

MESH = pl.DeviceIdType.MESH
BF16 = jnp.bfloat16
F32 = jnp.float32


def mm(a, b):
    return jnp.dot(a, b, preferred_element_type=F32)


def mm_nt(a, b):
    return lax.dot_general(a, b, (((1,), (1,)), ((), ())), preferred_element_type=F32)


def split_bf16(a):
    high = a.astype(BF16)
    return high, (a - high.astype(F32)).astype(BF16)


def remote(src, dst, send_sem, recv_sem, where):
    return pltpu.make_async_remote_copy(
        src_ref=src,
        dst_ref=dst,
        send_sem=send_sem,
        recv_sem=recv_sem,
        device_id=where,
        device_id_type=MESH,
    )


def x_partners(narrow):
    chip, core = narrow // 2, narrow % 2
    right = ((chip + 1) % CHIPS_X) * 2 + core
    left = ((chip + CHIPS_X - 1) % CHIPS_X) * 2 + core
    sibling = chip * 2 + 1 - core
    return chip, core, right, left, sibling


def kernel(
    blocks,
    rows,
    points,
    targets,
    centroids_hbm,
    block_list_hbm,
    lengths_hbm,
    sources_hbm,
    out,
    centroids,
    block_list,
    lengths,
    sources,
    own_p,
    own_t,
    sib_p,
    sib_t,
    res,
    res_sib,
    turned_t,
    kept,
    out_buf,
    in_buf,
    raw,
    hand_res,
    iterate,
    mine,
    rot,
    swap_out,
    swap_in0,
    swap_in1,
    hand0,
    hand1,
    got_z,
    got_y,
    pass_y,
    pass_z,
    last_y,
    last_z,
    ask,
    ask_y,
    ask_z,
    read_y,
    read_z,
    load_sem,
    swap_send,
    swap_recv,
    raw_send,
    raw_recv,
    gram_send,
    gram_recv,
    x_send,
    x_recv,
    rot_send,
    rot_recv,
    ask_sy,
    ask_sz,
    ask_ry,
    ask_rz,
    g_sz,
    g_rz,
    g_sy,
    g_ry,
    p_sy,
    p_ry,
    p_sz,
    p_rz,
    read_sem,
    near_sem,
):
    wide = lax.axis_index("wide")
    narrow = lax.axis_index("narrow")
    at_y, at_z = wide // RING_Z, wide % RING_Z
    chip, core, right, left, sibling = x_partners(narrow)
    right_chip = (chip + 1) % CHIPS_X
    left_chip = (chip + CHIPS_X - 1) % CHIPS_X
    opposite = (chip + 2) % CHIPS_X
    width = points.shape[1]
    total = blocks * rows
    handed = MOVE * rows

    def y_peer(step):
        other = (at_y + step) % RING_Y
        return other, {"wide": other * RING_Z + at_z}

    def z_peer(step):
        other = (at_z + step) % RING_Z
        return other, {"wide": at_y * RING_Z + other}

    y_steps = sorted(range(1, RING_Y), key=lambda s: -min(s, RING_Y - s))
    z_steps = sorted(range(1, RING_Z), key=lambda s: -min(s, RING_Z - s))
    around = (
        y_peer(1)[1],
        y_peer(RING_Y - 1)[1],
        z_peer(1)[1],
        z_peer(RING_Z - 1)[1],
    )

    barrier = pltpu.get_barrier_semaphore()
    for partner in (sibling, right, left):
        pl.semaphore_signal(barrier, inc=1, device_id={"narrow": partner}, device_id_type=MESH)
    for where in around:
        pl.semaphore_signal(barrier, inc=1, device_id=where, device_id_type=MESH)

    loads = [
        pltpu.make_async_copy(source, target, load_sem.at[index])
        for index, (source, target) in enumerate(
            (
                (targets, own_t),
                (points, own_p),
                (block_list_hbm, block_list),
                (lengths_hbm, lengths),
                (centroids_hbm, centroids),
                (sources_hbm, sources),
            )
        )
    ]
    for load in loads:
        load.start()
    pl.semaphore_wait(barrier, 3 + len(around))

    swap_t = remote(targets, sib_t, swap_send.at[0], swap_recv.at[0], {"narrow": sibling})
    swap_p = remote(points, sib_p, swap_send.at[1], swap_recv.at[1], {"narrow": sibling})
    swap_t.start()
    swap_p.start()
    sent = [swap_t, swap_p]

    raws = []

    def share_raw(src, owner, where):
        copy = remote(src, raw.at[owner], raw_send.at[len(raws)], raw_recv.at[owner], {"narrow": where})
        copy.start()
        raws.append(copy)

    def raw_arrived(owner):
        remote(
            raw.at[owner], raw.at[owner], raw_send.at[0], raw_recv.at[owner], {"narrow": sibling}
        ).wait_recv()

    share_raw(points.at[pl.ds(0, handed)], narrow, right)
    share_raw(points.at[pl.ds(0, handed)], narrow, left)

    def tell():
        for index, where in enumerate(around):
            pl.semaphore_signal(near_sem.at[index], inc=1, device_id=where, device_id_type=MESH)

    def tell_z():
        for index in (2, 3):
            pl.semaphore_signal(near_sem.at[index], inc=1, device_id=around[index], device_id_type=MESH)

    def hear(kinds):
        for index in kinds:
            pl.semaphore_wait(near_sem.at[index], 1)

    tell()

    def residual_of(value, block, first_row):
        centre = centroids[pl.ds(block_list[block], 1), :]
        row = first_row + lax.broadcasted_iota(jnp.int32, (rows, width), 0)
        return jnp.where(row < lengths[block], value.astype(F32) - centre, 0.0).astype(BF16)

    def residual_into(dst, src, first_row):
        def one(b, carry):
            here = pl.ds(pl.multiple_of(b * rows, rows), rows)
            dst[here, :] = residual_of(src[here, :], b, first_row)
            return carry

        lax.fori_loop(0, blocks, one, 0, unroll=4)

    def transpose_into(first, src):
        for piece in range(total // width):
            turned_t[:, first + piece * width : first + (piece + 1) * width] = src[
                piece * width : (piece + 1) * width, :
            ].T

    def half_gram(owner_chip, which, first, held):
        wanted = (owner_chip * 2 + core) * PER_DEV + which
        pieces = []
        for b in range(blocks):
            keep = jnp.where(block_list[b] == wanted, 1.0, 0.0).astype(BF16)
            pieces.append(held[b * rows : (b + 1) * rows, :] * keep)
        return mm(turned_t[:, first : first + total], jnp.concatenate(pieces, axis=0))

    def own_half(owner_chip, which):
        return half_gram(owner_chip, which, 0, res)

    def sib_half(owner_chip, which):
        return half_gram(owner_chip, which, total, res_sib)

    def hop(slot, where):
        return remote(
            out_buf.at[slot], in_buf.at[slot], gram_send.at[slot], gram_recv.at[slot], {"narrow": where}
        )

    hops = [hop(s, right if s % 2 == 0 else left) for s in range(6)]
    sent += hops
    early = ((opposite, 0), (opposite, 1), (right_chip, 1), (left_chip, 0))

    loads[0].wait()
    transpose_into(0, own_t)
    for load in loads[1:]:
        load.wait()
    residual_into(res, own_p, narrow * rows)
    for slot, (owner_chip, which) in enumerate(early):
        kept[slot] = own_half(owner_chip, which)
    swap_t.wait_recv()
    transpose_into(total, sib_t)
    swap_p.wait_recv()
    raw_arrived(left)
    share_raw(raw.at[left], left, right)
    residual_into(res_sib, sib_p, sibling * rows)

    def finish(slot):
        owner_chip, which = early[slot]
        out_buf[slot] = (kept[slot] + sib_half(owner_chip, which)).astype(BF16)
        hops[slot].start()

    finish(0)
    finish(1)
    hear((0, 1, 2, 3))
    tell()
    finish(2)
    share_raw(raw.at[left], left, sibling)
    raw_arrived(right)
    share_raw(raw.at[right], right, sibling)
    finish(3)
    hear((0, 1, 2, 3))
    tell()
    kept[0] = own_half(right_chip, 0) + sib_half(right_chip, 0)
    kept[1] = own_half(left_chip, 1) + sib_half(left_chip, 1)
    hops[0].wait_recv()
    out_buf[4] = (kept[0] + in_buf[0].astype(F32)).astype(BF16)
    hops[4].start()
    hops[1].wait_recv()
    out_buf[5] = (kept[1] + in_buf[1].astype(F32)).astype(BF16)
    hops[5].start()
    hear((0, 1, 2, 3))
    tell_z()
    across = opposite * 2 + core
    raw_arrived(across)
    share_raw(raw.at[across], across, sibling)
    kept[2] = own_half(chip, 0) + sib_half(chip, 0)
    hear((2, 3))
    tell_z()
    kept[3] = own_half(chip, 1) + sib_half(chip, 1)
    hear((2, 3))

    line = lax.broadcasted_iota(jnp.int32, ask.shape, 0)
    wish = jnp.where(line == 0, sources[0], sources[1])
    ask[...] = wish
    ask_y[at_y] = wish
    ask_z[at_z] = wish

    for step in y_steps:
        other, where = y_peer(step)
        copy = remote(ask, ask_y.at[at_y], ask_sy.at[step], ask_ry.at[at_y], where)
        copy.start()
        sent.append(copy)
    for step in z_steps:
        other, where = z_peer(step)
        copy = remote(ask, ask_z.at[at_z], ask_sz.at[step], ask_rz.at[at_z], where)
        copy.start()
        sent.append(copy)

    for b in range(MOVE):
        hand_res[b, pl.ds(pl.multiple_of(narrow * rows, rows), rows), :] = res[
            b * rows : (b + 1) * rows, :
        ]
        hand_res[b, pl.ds(pl.multiple_of(sibling * rows, rows), rows), :] = res_sib[
            b * rows : (b + 1) * rows, :
        ]
    for owner_chip in (left_chip, right_chip, opposite):
        raw_arrived(owner_chip * 2 + 1 - core)
        for owner_core in range(2):
            owner = owner_chip * 2 + owner_core
            for b in range(MOVE):
                hand_res[b, pl.ds(pl.multiple_of(owner * rows, rows), rows), :] = residual_of(
                    raw[owner, b * rows : (b + 1) * rows, :], b, owner * rows
                )

    hops[3].wait_recv()
    kept[2] = kept[2] + in_buf[3].astype(F32)
    hops[2].wait_recv()
    kept[3] = kept[3] + in_buf[2].astype(F32)
    hops[4].wait_recv()
    hops[5].wait_recv()
    for which in range(PER_DEV):
        total_gram = kept[2 + which] + in_buf[4 + which].astype(F32)
        norm = jnp.sqrt(jnp.sum(total_gram * total_gram, keepdims=True) + 1e-06)
        iterate[which] = total_gram * (1.0 / norm)

    def sweep(index, carry):
        for which in range(PER_DEV):
            held = iterate[which].astype(BF16)
            product = mm_nt(held, held).astype(BF16)
            iterate[which] = 1.5 * iterate[which] - 0.5 * mm(product, held)
        return carry

    lax.fori_loop(0, SWEEPS - 1, sweep, 0)
    for which in range(PER_DEV):
        exact = iterate[which]
        high, low = split_bf16(exact)
        product = mm_nt(high, high) + (mm_nt(high, low) + mm_nt(low, high))
        p_high, p_low = split_bf16(product)
        cubed = mm(p_high, high) + (mm(p_high, low) + mm(p_low, high))
        rotation = (1.5 * exact - 0.5 * cubed).astype(BF16)
        mine[which] = rotation
        rot[narrow * PER_DEV + which] = rotation

    swap_in = (swap_in0, swap_in1)
    x_peers = []
    for chip_step, flip in ((2, 0), (2, 1), (1, 0), (1, 1), (3, 0), (3, 1), (0, 1)):
        peer_core = core + flip - 2 * core * flip
        x_peers.append(((chip + chip_step) % CHIPS_X) * 2 + peer_core)
    for b in range(MOVE):
        chosen = mine[block_list[b] % PER_DEV]
        swap_out[b] = mm_nt(hand_res[b], chosen).astype(BF16).reshape(2 * CHIPS_X, rows, width)
        swap_in[b][narrow] = swap_out[b, narrow]
        for peer in x_peers:
            copy = remote(
                swap_out.at[b, peer],
                swap_in[b].at[narrow],
                x_send.at[b, peer],
                x_recv.at[b, narrow],
                {"narrow": peer},
            )
            copy.start()
            sent.append(copy)

    def x_arrived(b):
        for peer in x_peers:
            remote(
                swap_out.at[b, peer], swap_in[b].at[peer], x_send.at[b, peer], x_recv.at[b, peer], {"narrow": peer}
            ).wait_recv()

    def place(owner_chip, owner_core, which):
        return (owner_chip * 2 + owner_core) * PER_DEV + which

    shares = []

    def share(slot, where):
        copy = remote(
            rot.at[slot], rot.at[slot], rot_send.at[len(shares)], rot_recv.at[slot], {"narrow": where}
        )
        copy.start()
        shares.append(copy)

    def arrived(slot):
        remote(rot.at[slot], rot.at[slot], rot_send.at[0], rot_recv.at[slot], {"narrow": sibling}).wait_recv()

    share(place(chip, core, 1), left)
    share(place(chip, core, 0), left)
    share(place(chip, core, 0), sibling)
    share(place(chip, core, 1), sibling)

    for step in y_steps:
        other, where = y_peer(step)
        remote(ask, ask_y.at[other], ask_sy.at[step], ask_ry.at[other], where).wait_recv()
    for step in z_steps:
        other, where = z_peer(step)
        remote(ask, ask_z.at[other], ask_sz.at[step], ask_rz.at[other], where).wait_recv()
    to_scalars_y = pltpu.make_async_copy(ask_y, read_y, read_sem.at[0])
    to_scalars_z = pltpu.make_async_copy(ask_z, read_z, read_sem.at[1])
    to_scalars_y.start()
    to_scalars_z.start()
    to_scalars_y.wait()
    to_scalars_z.wait()

    x_arrived(0)
    first = swap_in0[block_list[0] // PER_DEV]
    hand0[...] = first
    got_z[at_z] = first
    for step in z_steps:
        other, where = z_peer(step)
        copy = remote(hand0, got_z.at[at_z], g_sz.at[step], g_rz.at[at_z], where)
        copy.start()
        sent.append(copy)
    share(place(chip, core, 0), right)
    share(place(chip, core, 1), right)
    x_arrived(1)
    second = swap_in1[block_list[1] // PER_DEV]
    hand1[...] = second
    got_y[at_y] = second
    for step in y_steps:
        other, where = y_peer(step)
        copy = remote(hand1, got_y.at[at_y], g_sy.at[step], g_ry.at[at_y], where)
        copy.start()
        sent.append(copy)

    def z_arrived(step):
        other, where = z_peer(step)
        remote(hand0, got_z.at[other], g_sz.at[step], g_rz.at[other], where).wait_recv()

    def share_if(here, slot, where, index):
        copy = remote(
            rot.at[slot], rot.at[slot], rot_send.at[index], rot_recv.at[slot], {"narrow": where}
        )

        @pl.when(here)
        def _():
            copy.start()

        return copy

    arrived(place(right_chip, core, 1))
    share(place(right_chip, core, 1), left)
    share(place(right_chip, core, 1), sibling)

    arrived(place(left_chip, core, 0))
    share_if(core == 0, place(left_chip, core, 0), right, 14)
    share(place(left_chip, core, 0), sibling)

    def turn(b):
        base = pl.multiple_of(b * rows, rows)
        return mm_nt(res[pl.ds(base, rows), :], rot[block_list[b]]).astype(BF16)

    def from_y(source):
        return source // blocks // RING_Z

    def from_z(source):
        return source // blocks % RING_Z

    for step in y_steps:
        other, where = y_peer(step)
        remote(hand1, got_y.at[other], g_sy.at[step], g_ry.at[other], where).wait_recv()
    last_z[at_z] = got_y[from_y(sources[1])]
    for step in z_steps:
        other, where = z_peer(step)
        pass_z[other] = got_y[from_y(read_z[other, 1, 0])]
        copy = remote(pass_z.at[other], last_z.at[at_z], p_sz.at[step], p_rz.at[at_z], where)
        copy.start()
        sent.append(copy)

    arrived(place(right_chip, core, 0))
    odd_relay = share_if(core == 1, place(right_chip, core, 0), left, 14)
    share(place(right_chip, core, 0), sibling)
    arrived(place(left_chip, core, 1))
    share(place(left_chip, core, 1), sibling)

    for step in z_steps:
        z_arrived(step)
    last_y[at_y] = got_z[from_z(sources[0])]
    for step in y_steps:
        other, where = y_peer(step)
        pass_y[other] = got_z[from_z(read_y[other, 0, 0])]
        copy = remote(pass_y.at[other], last_y.at[at_y], p_sy.at[step], p_ry.at[at_y], where)
        copy.start()
        sent.append(copy)

    arrived(place(opposite, core, 1))
    share(place(opposite, core, 1), sibling)
    arrived(place(opposite, core, 0))
    share(place(opposite, core, 0), sibling)
    for owner_chip in (chip, left_chip, right_chip, opposite):
        for which in range(PER_DEV):
            arrived(place(owner_chip, 1 - core, which))

    def turn_one(b, carry):
        out[pl.ds(pl.multiple_of(b * rows, rows), rows), :] = turn(b)
        return carry

    lax.fori_loop(MOVE, blocks, turn_one, 0, unroll=6)

    for step in y_steps:
        other, where = y_peer(step)
        remote(hand1, last_y.at[other], p_sy.at[step], p_ry.at[other], where).wait_recv()
    out[0:rows, :] = last_y[from_y(sources[0])]
    for step in z_steps:
        other, where = z_peer(step)
        remote(hand0, last_z.at[other], p_sz.at[step], p_rz.at[other], where).wait_recv()
    out[rows : 2 * rows, :] = last_z[from_z(sources[1])]

    for copy in sent + raws + shares + [odd_relay]:
        copy.wait_send()


def local(points, targets, centroids, block_list, lengths, sources):
    blocks, rows, width = points.shape
    lists = centroids.shape[0]
    total = blocks * rows
    narrow_size = 2 * CHIPS_X
    hbm = pl.BlockSpec(memory_space=pltpu.HBM)
    dma = pltpu.SemaphoreType.DMA
    square = (width, width)
    tile = (rows, width)
    ask = (8, 128)
    rotated = pl.pallas_call(
        functools.partial(kernel, blocks, rows),
        out_shape=pltpu.VMEM((total, width), BF16),
        in_specs=[hbm] * 6,
        out_specs=pl.BlockSpec(memory_space=pltpu.VMEM),
        scratch_shapes=[
            pltpu.VMEM(centroids.shape, F32),
            pltpu.SMEM((blocks,), jnp.int32),
            pltpu.SMEM((blocks,), jnp.int32),
            pltpu.SMEM((blocks,), jnp.int32),
            *[pltpu.VMEM((total, width), BF16)] * 6,
            pltpu.VMEM((width, 2 * total), BF16),
            pltpu.VMEM((4, *square), F32),
            pltpu.VMEM((6, *square), BF16),
            pltpu.VMEM((6, *square), BF16),
            pltpu.VMEM((narrow_size, MOVE * rows, width), BF16),
            pltpu.VMEM((MOVE, narrow_size * rows, width), BF16),
            pltpu.VMEM((PER_DEV, *square), F32),
            pltpu.VMEM((PER_DEV, *square), BF16),
            pltpu.VMEM((lists, *square), BF16),
            pltpu.VMEM((MOVE, narrow_size, rows, width), BF16),
            pltpu.VMEM((narrow_size, rows, width), BF16),
            pltpu.VMEM((narrow_size, rows, width), BF16),
            pltpu.VMEM(tile, BF16),
            pltpu.VMEM(tile, BF16),
            pltpu.VMEM((RING_Z, *tile), BF16),
            pltpu.VMEM((RING_Y, *tile), BF16),
            pltpu.VMEM((RING_Y, *tile), BF16),
            pltpu.VMEM((RING_Z, *tile), BF16),
            pltpu.VMEM((RING_Y, *tile), BF16),
            pltpu.VMEM((RING_Z, *tile), BF16),
            pltpu.VMEM(ask, jnp.int32),
            pltpu.VMEM((RING_Y, *ask), jnp.int32),
            pltpu.VMEM((RING_Z, *ask), jnp.int32),
            pltpu.SMEM((RING_Y, *ask), jnp.int32),
            pltpu.SMEM((RING_Z, *ask), jnp.int32),
            dma((6,)),
            dma((2,)),
            dma((2,)),
            dma((6,)),
            dma((narrow_size,)),
            dma((6,)),
            dma((6,)),
            dma((MOVE, narrow_size)),
            dma((MOVE, narrow_size)),
            dma((15,)),
            dma((lists,)),
            dma((RING_Y,)),
            dma((RING_Z,)),
            dma((RING_Y,)),
            dma((RING_Z,)),
            dma((RING_Z,)),
            dma((RING_Z,)),
            dma((RING_Y,)),
            dma((RING_Y,)),
            dma((RING_Y,)),
            dma((RING_Y,)),
            dma((RING_Z,)),
            dma((RING_Z,)),
            dma((2,)),
            pltpu.SemaphoreType.REGULAR((4,)),
        ],
        compiler_params=pltpu.CompilerParams(
            collective_id=0, has_side_effects=True, vmem_limit_bytes=60 << 20
        ),
        name="rotate_lists",
    )(
        points.reshape(total, width),
        targets.reshape(total, width),
        centroids,
        block_list,
        lengths,
        sources,
    )
    return rotated.reshape(blocks, rows, width)


def solution(mesh):
    return jax.shard_map(
        local,
        mesh=mesh,
        in_specs=(
            P("wide", "narrow", None),
            P("wide", "narrow", None),
            P("wide", None),
            P("wide"),
            P("wide"),
            P("wide"),
        ),
        out_specs=P("wide", "narrow", None),
        check_vma=False,
    )
```

```python
import functools

import jax
import jax.numpy as jnp
from jax import lax
from jax.experimental import pallas as pl
from jax.experimental.pallas import tpu as pltpu
from jax.sharding import PartitionSpec as P

MOVE = 2
SWEEPS = 5
CHIPS_X = 4
RING_Y = 8
RING_Z = 12
PER_DEV = 2

MESH = pl.DeviceIdType.MESH
BF16 = jnp.bfloat16
F32 = jnp.float32


def mm(a, b):
    return jnp.dot(a, b, preferred_element_type=F32)


def mm_nt(a, b):
    return lax.dot_general(a, b, (((1,), (1,)), ((), ())), preferred_element_type=F32)


def split_bf16(a):
    high = a.astype(BF16)
    return high, (a - high.astype(F32)).astype(BF16)


def remote(src, dst, send_sem, recv_sem, where):
    return pltpu.make_async_remote_copy(
        src_ref=src,
        dst_ref=dst,
        send_sem=send_sem,
        recv_sem=recv_sem,
        device_id=where,
        device_id_type=MESH,
    )


def x_partners(narrow):
    chip, core = narrow // 2, narrow % 2
    right = ((chip + 1) % CHIPS_X) * 2 + core
    left = ((chip + CHIPS_X - 1) % CHIPS_X) * 2 + core
    sibling = chip * 2 + 1 - core
    return chip, core, right, left, sibling


def kernel(
    blocks,
    rows,
    points,
    targets,
    centroids_hbm,
    block_list_hbm,
    lengths_hbm,
    sources_hbm,
    out,
    centroids,
    block_list,
    lengths,
    sources,
    own_p,
    own_t,
    sib_p,
    sib_t,
    res,
    res_sib,
    turned_t,
    kept,
    out_buf,
    in_buf,
    raw,
    hand_res,
    iterate,
    mine,
    rot,
    swap_out,
    swap_in0,
    swap_in1,
    hand0,
    hand1,
    got_z,
    got_y,
    pass_y,
    pass_z,
    last_y,
    last_z,
    ask,
    ask_y,
    ask_z,
    read_y,
    read_z,
    load_sem,
    swap_send,
    swap_recv,
    raw_send,
    raw_recv,
    gram_send,
    gram_recv,
    x_send,
    x_recv,
    rot_send,
    rot_recv,
    ask_sy,
    ask_sz,
    ask_ry,
    ask_rz,
    g_sz,
    g_rz,
    g_sy,
    g_ry,
    p_sy,
    p_ry,
    p_sz,
    p_rz,
    read_sem,
    near_sem,
):
    wide = lax.axis_index("wide")
    narrow = lax.axis_index("narrow")
    at_y, at_z = wide // RING_Z, wide % RING_Z
    chip, core, right, left, sibling = x_partners(narrow)
    right_chip = (chip + 1) % CHIPS_X
    left_chip = (chip + CHIPS_X - 1) % CHIPS_X
    opposite = (chip + 2) % CHIPS_X
    width = points.shape[1]
    total = blocks * rows
    handed = MOVE * rows

    def y_peer(step):
        other = (at_y + step) % RING_Y
        return other, {"wide": other * RING_Z + at_z}

    def z_peer(step):
        other = (at_z + step) % RING_Z
        return other, {"wide": at_y * RING_Z + other}

    y_steps = sorted(range(1, RING_Y), key=lambda s: -min(s, RING_Y - s))
    z_steps = sorted(range(1, RING_Z), key=lambda s: -min(s, RING_Z - s))
    around = (
        y_peer(1)[1],
        y_peer(RING_Y - 1)[1],
        z_peer(1)[1],
        z_peer(RING_Z - 1)[1],
    )

    barrier = pltpu.get_barrier_semaphore()
    for partner in (sibling, right, left):
        pl.semaphore_signal(barrier, inc=1, device_id={"narrow": partner}, device_id_type=MESH)
    for where in around:
        pl.semaphore_signal(barrier, inc=1, device_id=where, device_id_type=MESH)

    loads = [
        pltpu.make_async_copy(source, target, load_sem.at[index])
        for index, (source, target) in enumerate(
            (
                (targets, own_t),
                (points, own_p),
                (block_list_hbm, block_list),
                (lengths_hbm, lengths),
                (centroids_hbm, centroids),
                (sources_hbm, sources),
            )
        )
    ]
    for load in loads:
        load.start()
    pl.semaphore_wait(barrier, 3 + len(around))

    swap_t = remote(targets, sib_t, swap_send.at[0], swap_recv.at[0], {"narrow": sibling})
    swap_p = remote(points, sib_p, swap_send.at[1], swap_recv.at[1], {"narrow": sibling})
    swap_t.start()
    swap_p.start()
    sent = [swap_t, swap_p]

    raws = []

    def share_raw(src, owner, where):
        copy = remote(src, raw.at[owner], raw_send.at[len(raws)], raw_recv.at[owner], {"narrow": where})
        copy.start()
        raws.append(copy)

    def raw_arrived(owner):
        remote(
            raw.at[owner], raw.at[owner], raw_send.at[0], raw_recv.at[owner], {"narrow": sibling}
        ).wait_recv()

    share_raw(points.at[pl.ds(0, handed)], narrow, right)
    share_raw(points.at[pl.ds(0, handed)], narrow, left)

    def tell():
        for index, where in enumerate(around):
            pl.semaphore_signal(near_sem.at[index], inc=1, device_id=where, device_id_type=MESH)

    def tell_z():
        for index in (2, 3):
            pl.semaphore_signal(near_sem.at[index], inc=1, device_id=around[index], device_id_type=MESH)

    def hear(kinds):
        for index in kinds:
            pl.semaphore_wait(near_sem.at[index], 1)

    tell()

    def residual_of(value, block, first_row):
        centre = centroids[pl.ds(block_list[block], 1), :]
        row = first_row + lax.broadcasted_iota(jnp.int32, (rows, width), 0)
        return jnp.where(row < lengths[block], value.astype(F32) - centre, 0.0).astype(BF16)

    def residual_into(dst, src, first_row):
        def one(b, carry):
            here = pl.ds(pl.multiple_of(b * rows, rows), rows)
            dst[here, :] = residual_of(src[here, :], b, first_row)
            return carry

        lax.fori_loop(0, blocks, one, 0, unroll=4)

    def transpose_into(first, src):
        for piece in range(total // width):
            turned_t[:, first + piece * width : first + (piece + 1) * width] = src[
                piece * width : (piece + 1) * width, :
            ].T

    def half_gram(owner_chip, which, first, held):
        wanted = (owner_chip * 2 + core) * PER_DEV + which
        pieces = []
        for b in range(blocks):
            keep = jnp.where(block_list[b] == wanted, 1.0, 0.0).astype(BF16)
            pieces.append(held[b * rows : (b + 1) * rows, :] * keep)
        return mm(turned_t[:, first : first + total], jnp.concatenate(pieces, axis=0))

    def own_half(owner_chip, which):
        return half_gram(owner_chip, which, 0, res)

    def sib_half(owner_chip, which):
        return half_gram(owner_chip, which, total, res_sib)

    def hop(slot, where):
        return remote(
            out_buf.at[slot], in_buf.at[slot], gram_send.at[slot], gram_recv.at[slot], {"narrow": where}
        )

    hops = [hop(s, right if s % 2 == 0 else left) for s in range(6)]
    sent += hops
    early = ((opposite, 0), (opposite, 1), (right_chip, 1), (left_chip, 0))

    loads[0].wait()
    transpose_into(0, own_t)
    for load in loads[1:]:
        load.wait()
    residual_into(res, own_p, narrow * rows)
    for slot, (owner_chip, which) in enumerate(early):
        kept[slot] = own_half(owner_chip, which)
    swap_t.wait_recv()
    transpose_into(total, sib_t)
    swap_p.wait_recv()
    raw_arrived(left)
    share_raw(raw.at[left], left, right)
    residual_into(res_sib, sib_p, sibling * rows)

    def finish(slot):
        owner_chip, which = early[slot]
        out_buf[slot] = (kept[slot] + sib_half(owner_chip, which)).astype(BF16)
        hops[slot].start()

    finish(0)
    finish(1)
    hear((0, 1, 2, 3))
    tell()
    finish(2)
    share_raw(raw.at[left], left, sibling)
    raw_arrived(right)
    share_raw(raw.at[right], right, sibling)
    finish(3)
    hear((0, 1, 2, 3))
    tell()
    kept[0] = own_half(right_chip, 0) + sib_half(right_chip, 0)
    kept[1] = own_half(left_chip, 1) + sib_half(left_chip, 1)
    hops[0].wait_recv()
    out_buf[4] = (kept[0] + in_buf[0].astype(F32)).astype(BF16)
    hops[4].start()
    hops[1].wait_recv()
    out_buf[5] = (kept[1] + in_buf[1].astype(F32)).astype(BF16)
    hops[5].start()
    hear((0, 1, 2, 3))
    tell_z()
    across = opposite * 2 + core
    raw_arrived(across)
    share_raw(raw.at[across], across, sibling)
    kept[2] = own_half(chip, 0) + sib_half(chip, 0)
    hear((2, 3))
    tell_z()
    kept[3] = own_half(chip, 1) + sib_half(chip, 1)
    hear((2, 3))

    line = lax.broadcasted_iota(jnp.int32, ask.shape, 0)
    wish = jnp.where(line == 0, sources[0], sources[1])
    ask[...] = wish
    ask_y[at_y] = wish
    ask_z[at_z] = wish

    for step in y_steps:
        other, where = y_peer(step)
        copy = remote(ask, ask_y.at[at_y], ask_sy.at[step], ask_ry.at[at_y], where)
        copy.start()
        sent.append(copy)
    for step in z_steps:
        other, where = z_peer(step)
        copy = remote(ask, ask_z.at[at_z], ask_sz.at[step], ask_rz.at[at_z], where)
        copy.start()
        sent.append(copy)

    for b in range(MOVE):
        hand_res[b, pl.ds(pl.multiple_of(narrow * rows, rows), rows), :] = res[
            b * rows : (b + 1) * rows, :
        ]
        hand_res[b, pl.ds(pl.multiple_of(sibling * rows, rows), rows), :] = res_sib[
            b * rows : (b + 1) * rows, :
        ]
    for owner_chip in (left_chip, right_chip, opposite):
        raw_arrived(owner_chip * 2 + 1 - core)
        for owner_core in range(2):
            owner = owner_chip * 2 + owner_core
            for b in range(MOVE):
                hand_res[b, pl.ds(pl.multiple_of(owner * rows, rows), rows), :] = residual_of(
                    raw[owner, b * rows : (b + 1) * rows, :], b, owner * rows
                )

    hops[3].wait_recv()
    kept[2] = kept[2] + in_buf[3].astype(F32)
    hops[2].wait_recv()
    kept[3] = kept[3] + in_buf[2].astype(F32)
    hops[4].wait_recv()
    hops[5].wait_recv()
    for which in range(PER_DEV):
        total_gram = kept[2 + which] + in_buf[4 + which].astype(F32)
        norm = jnp.sqrt(jnp.sum(total_gram * total_gram, keepdims=True) + 1e-06)
        iterate[which] = total_gram * (1.0 / norm)

    def sweep(index, carry):
        for which in range(PER_DEV):
            held = iterate[which].astype(BF16)
            product = mm_nt(held, held).astype(BF16)
            iterate[which] = 1.5 * iterate[which] - 0.5 * mm(product, held)
        return carry

    lax.fori_loop(0, SWEEPS - 1, sweep, 0)
    for which in range(PER_DEV):
        exact = iterate[which]
        high, low = split_bf16(exact)
        product = mm_nt(high, high) + (mm_nt(high, low) + mm_nt(low, high))
        p_high, p_low = split_bf16(product)
        cubed = mm(p_high, high) + (mm(p_high, low) + mm(p_low, high))
        rotation = (1.5 * exact - 0.5 * cubed).astype(BF16)
        mine[which] = rotation
        rot[narrow * PER_DEV + which] = rotation

    swap_in = (swap_in0, swap_in1)
    x_peers = []
    for chip_step, flip in ((2, 0), (2, 1), (1, 0), (1, 1), (3, 0), (3, 1), (0, 1)):
        peer_core = core + flip - 2 * core * flip
        x_peers.append(((chip + chip_step) % CHIPS_X) * 2 + peer_core)
    for b in range(MOVE):
        chosen = mine[block_list[b] % PER_DEV]
        swap_out[b] = mm_nt(hand_res[b], chosen).astype(BF16).reshape(2 * CHIPS_X, rows, width)
        swap_in[b][narrow] = swap_out[b, narrow]
        for peer in x_peers:
            copy = remote(
                swap_out.at[b, peer],
                swap_in[b].at[narrow],
                x_send.at[b, peer],
                x_recv.at[b, narrow],
                {"narrow": peer},
            )
            copy.start()
            sent.append(copy)

    def x_arrived(b):
        for peer in x_peers:
            remote(
                swap_out.at[b, peer], swap_in[b].at[peer], x_send.at[b, peer], x_recv.at[b, peer], {"narrow": peer}
            ).wait_recv()

    def place(owner_chip, owner_core, which):
        return (owner_chip * 2 + owner_core) * PER_DEV + which

    shares = []

    def share(slot, where):
        copy = remote(
            rot.at[slot], rot.at[slot], rot_send.at[len(shares)], rot_recv.at[slot], {"narrow": where}
        )
        copy.start()
        shares.append(copy)

    def arrived(slot):
        remote(rot.at[slot], rot.at[slot], rot_send.at[0], rot_recv.at[slot], {"narrow": sibling}).wait_recv()

    share(place(chip, core, 1), left)
    share(place(chip, core, 0), left)
    share(place(chip, core, 0), sibling)
    share(place(chip, core, 1), sibling)

    for step in y_steps:
        other, where = y_peer(step)
        remote(ask, ask_y.at[other], ask_sy.at[step], ask_ry.at[other], where).wait_recv()
    for step in z_steps:
        other, where = z_peer(step)
        remote(ask, ask_z.at[other], ask_sz.at[step], ask_rz.at[other], where).wait_recv()
    to_scalars_y = pltpu.make_async_copy(ask_y, read_y, read_sem.at[0])
    to_scalars_z = pltpu.make_async_copy(ask_z, read_z, read_sem.at[1])
    to_scalars_y.start()
    to_scalars_z.start()
    to_scalars_y.wait()
    to_scalars_z.wait()

    x_arrived(0)
    first = swap_in0[block_list[0] // PER_DEV]
    hand0[...] = first
    got_z[at_z] = first
    for step in z_steps:
        other, where = z_peer(step)
        copy = remote(hand0, got_z.at[at_z], g_sz.at[step], g_rz.at[at_z], where)
        copy.start()
        sent.append(copy)
    share(place(chip, core, 0), right)
    share(place(chip, core, 1), right)
    x_arrived(1)
    second = swap_in1[block_list[1] // PER_DEV]
    hand1[...] = second
    got_y[at_y] = second
    for step in y_steps:
        other, where = y_peer(step)
        copy = remote(hand1, got_y.at[at_y], g_sy.at[step], g_ry.at[at_y], where)
        copy.start()
        sent.append(copy)

    def z_arrived(step):
        other, where = z_peer(step)
        remote(hand0, got_z.at[other], g_sz.at[step], g_rz.at[other], where).wait_recv()

    def share_if(here, slot, where, index):
        copy = remote(
            rot.at[slot], rot.at[slot], rot_send.at[index], rot_recv.at[slot], {"narrow": where}
        )

        @pl.when(here)
        def _():
            copy.start()

        return copy

    arrived(place(right_chip, core, 1))
    share(place(right_chip, core, 1), left)
    share(place(right_chip, core, 1), sibling)

    arrived(place(left_chip, core, 0))
    share_if(core == 0, place(left_chip, core, 0), right, 14)
    share(place(left_chip, core, 0), sibling)
    arrived(place(right_chip, core, 0))
    odd_relay = share_if(core == 1, place(right_chip, core, 0), left, 14)
    share(place(right_chip, core, 0), sibling)

    def turn(b):
        base = pl.multiple_of(b * rows, rows)
        return mm_nt(res[pl.ds(base, rows), :], rot[block_list[b]]).astype(BF16)

    def from_y(source):
        return source // blocks // RING_Z

    def from_z(source):
        return source // blocks % RING_Z

    for step in y_steps:
        other, where = y_peer(step)
        remote(hand1, got_y.at[other], g_sy.at[step], g_ry.at[other], where).wait_recv()
    last_z[at_z] = got_y[from_y(sources[1])]
    for step in z_steps:
        other, where = z_peer(step)
        pass_z[other] = got_y[from_y(read_z[other, 1, 0])]
        copy = remote(pass_z.at[other], last_z.at[at_z], p_sz.at[step], p_rz.at[at_z], where)
        copy.start()
        sent.append(copy)

    for step in z_steps:
        z_arrived(step)
    last_y[at_y] = got_z[from_z(sources[0])]
    for step in y_steps:
        other, where = y_peer(step)
        pass_y[other] = got_z[from_z(read_y[other, 0, 0])]
        copy = remote(pass_y.at[other], last_y.at[at_y], p_sy.at[step], p_ry.at[at_y], where)
        copy.start()
        sent.append(copy)

    arrived(place(left_chip, core, 1))
    share(place(left_chip, core, 1), sibling)
    arrived(place(opposite, core, 1))
    share(place(opposite, core, 1), sibling)
    arrived(place(opposite, core, 0))
    share(place(opposite, core, 0), sibling)
    for owner_chip in (chip, left_chip, right_chip, opposite):
        for which in range(PER_DEV):
            arrived(place(owner_chip, 1 - core, which))

    def turn_one(b, carry):
        out[pl.ds(pl.multiple_of(b * rows, rows), rows), :] = turn(b)
        return carry

    lax.fori_loop(MOVE, blocks, turn_one, 0, unroll=6)

    for step in y_steps:
        other, where = y_peer(step)
        remote(hand1, last_y.at[other], p_sy.at[step], p_ry.at[other], where).wait_recv()
    out[0:rows, :] = last_y[from_y(sources[0])]
    for step in z_steps:
        other, where = z_peer(step)
        remote(hand0, last_z.at[other], p_sz.at[step], p_rz.at[other], where).wait_recv()
    out[rows : 2 * rows, :] = last_z[from_z(sources[1])]

    for copy in sent + raws + shares + [odd_relay]:
        copy.wait_send()


def local(points, targets, centroids, block_list, lengths, sources):
    blocks, rows, width = points.shape
    lists = centroids.shape[0]
    total = blocks * rows
    narrow_size = 2 * CHIPS_X
    hbm = pl.BlockSpec(memory_space=pltpu.HBM)
    dma = pltpu.SemaphoreType.DMA
    square = (width, width)
    tile = (rows, width)
    ask = (8, 128)
    rotated = pl.pallas_call(
        functools.partial(kernel, blocks, rows),
        out_shape=pltpu.VMEM((total, width), BF16),
        in_specs=[hbm] * 6,
        out_specs=pl.BlockSpec(memory_space=pltpu.VMEM),
        scratch_shapes=[
            pltpu.VMEM(centroids.shape, F32),
            pltpu.SMEM((blocks,), jnp.int32),
            pltpu.SMEM((blocks,), jnp.int32),
            pltpu.SMEM((blocks,), jnp.int32),
            *[pltpu.VMEM((total, width), BF16)] * 6,
            pltpu.VMEM((width, 2 * total), BF16),
            pltpu.VMEM((4, *square), F32),
            pltpu.VMEM((6, *square), BF16),
            pltpu.VMEM((6, *square), BF16),
            pltpu.VMEM((narrow_size, MOVE * rows, width), BF16),
            pltpu.VMEM((MOVE, narrow_size * rows, width), BF16),
            pltpu.VMEM((PER_DEV, *square), F32),
            pltpu.VMEM((PER_DEV, *square), BF16),
            pltpu.VMEM((lists, *square), BF16),
            pltpu.VMEM((MOVE, narrow_size, rows, width), BF16),
            pltpu.VMEM((narrow_size, rows, width), BF16),
            pltpu.VMEM((narrow_size, rows, width), BF16),
            pltpu.VMEM(tile, BF16),
            pltpu.VMEM(tile, BF16),
            pltpu.VMEM((RING_Z, *tile), BF16),
            pltpu.VMEM((RING_Y, *tile), BF16),
            pltpu.VMEM((RING_Y, *tile), BF16),
            pltpu.VMEM((RING_Z, *tile), BF16),
            pltpu.VMEM((RING_Y, *tile), BF16),
            pltpu.VMEM((RING_Z, *tile), BF16),
            pltpu.VMEM(ask, jnp.int32),
            pltpu.VMEM((RING_Y, *ask), jnp.int32),
            pltpu.VMEM((RING_Z, *ask), jnp.int32),
            pltpu.SMEM((RING_Y, *ask), jnp.int32),
            pltpu.SMEM((RING_Z, *ask), jnp.int32),
            dma((6,)),
            dma((2,)),
            dma((2,)),
            dma((6,)),
            dma((narrow_size,)),
            dma((6,)),
            dma((6,)),
            dma((MOVE, narrow_size)),
            dma((MOVE, narrow_size)),
            dma((15,)),
            dma((lists,)),
            dma((RING_Y,)),
            dma((RING_Z,)),
            dma((RING_Y,)),
            dma((RING_Z,)),
            dma((RING_Z,)),
            dma((RING_Z,)),
            dma((RING_Y,)),
            dma((RING_Y,)),
            dma((RING_Y,)),
            dma((RING_Y,)),
            dma((RING_Z,)),
            dma((RING_Z,)),
            dma((2,)),
            pltpu.SemaphoreType.REGULAR((4,)),
        ],
        compiler_params=pltpu.CompilerParams(
            collective_id=0, has_side_effects=True, vmem_limit_bytes=60 << 20
        ),
        name="rotate_lists",
    )(
        points.reshape(total, width),
        targets.reshape(total, width),
        centroids,
        block_list,
        lengths,
        sources,
    )
    return rotated.reshape(blocks, rows, width)


def solution(mesh):
    return jax.shard_map(
        local,
        mesh=mesh,
        in_specs=(
            P("wide", "narrow", None),
            P("wide", "narrow", None),
            P("wide", None),
            P("wide"),
            P("wide"),
            P("wide"),
        ),
        out_specs=P("wide", "narrow", None),
        check_vma=False,
    )
```
